256 devices in a mesh: gx: 8 (over y, core), gy: 4 (over x), gz: 8 (over z).
Axes of the slice: x: 4, y: 4, z: 8, core: 2. Of those that a mesh axis runs over, the one named last changes fastest.
Arguments:
- magnetic: float32 [3, 128, 128, 1024], P(None, 'gx', 'gy', 'gz'), may hold values from -11 to 11
Outputs:
- cleaned: float32 [3, 128, 128, 1024], P(None, 'gx', 'gy', 'gz')
The draws below stay inside these ranges and needn't reach their ends.
All inputs are finite; a program needn't handle non-finite values.
Results may differ from the reference program's by a relative error of at most 0.00018.
Values sent between devices are 32-bit elements; how exact they have to be, the bound alone decides.
A program may use at most 128 MiB of HBM per device.

```python
import math
import jax
import jax.numpy as jnp
from jax import lax

LEVELS = 5
SWEEPS = 3
COARSE_ITERS = 24
NX = 128
NY = 128
NZ = 1024


def smooth_profile(key, extent, low_amp, high_amp):
    position_line = jnp.arange(extent).astype(jnp.float32)
    profile = jnp.zeros((extent,), jnp.float32)
    for level_order in range(3):
        period_cells = 2 ** (LEVELS - 1) * 2 ** (3 - level_order)
        wave_count = max(1, extent // period_cells)
        amp_key, shift_key, sign_key = jax.random.split(jax.random.fold_in(key, level_order), 3)
        amplitude = jax.random.uniform(amp_key, (), jnp.float32, low_amp, high_amp)
        sign_value = jnp.where(jax.random.bernoulli(sign_key), 1.0, -1.0).astype(jnp.float32)
        phase_shift = jax.random.uniform(shift_key, (), jnp.float32, 0.0, 2.0 * math.pi)
        angle_line = 2.0 * math.pi * wave_count * position_line / extent + phase_shift
        profile = profile + sign_value * amplitude * jnp.sin(angle_line)
    return profile


def draw_magnetic(key, part):
    noise_key, smooth_key = jax.random.split(key, 2)
    extents = (NX, NY, NZ)
    noise_field = jnp.clip(jax.random.normal(noise_key, (3, NX, NY, NZ), jnp.float32), -6.0, 6.0)
    low_amp, high_amp = (0.6, 1.2)
    pieces = []
    for component in range(3):
        profile = smooth_profile(jax.random.fold_in(smooth_key, component), extents[component], low_amp, high_amp)
        shape_list = [1, 1, 1]
        shape_list[component] = extents[component]
        pieces.append(noise_field[component] + profile.reshape(shape_list))
    return jnp.stack(pieces).astype(jnp.float32)


def setup_inputs(seed: int = 0) -> dict:
    splits = jax.random.split(jax.random.key(seed), 2)
    magnetic = draw_magnetic(jax.random.fold_in(splits[1], 71), 0)
    return {"magnetic": magnetic}


relax_weight = 6.0 / 7.0


def apply_local(values, stretch):
    beside = jnp.roll(values, -1, 0) + jnp.roll(values, 1, 0)
    beside = beside + jnp.roll(values, -1, 1) + jnp.roll(values, 1, 1)
    beside = beside + jnp.roll(values, -1, 2) + jnp.roll(values, 1, 2)
    return (6.0 * values - beside) * stretch


def restrict(values):
    extent = values.shape
    blocks = values.reshape(extent[0] // 2, 2, extent[1] // 2, 2, extent[2] // 2, 2)
    return jnp.sum(blocks, axis=(1, 3, 5)) * 0.125


def prolong(values):
    extent = values.shape
    spread = jnp.broadcast_to(values[:, None, :, None, :, None], (extent[0], 2, extent[1], 2, extent[2], 2))
    return spread.reshape(extent[0] * 2, extent[1] * 2, extent[2] * 2)


def cycle_whole(source, level_index):
    stretch = 0.25 ** level_index
    factor = relax_weight * 4.0 ** level_index / 6.0
    solution = factor * source
    if level_index == LEVELS - 1:
        def coarse_sweep(iteration, current):
            return current + factor * (source - apply_local(current, stretch))
        return lax.fori_loop(0, COARSE_ITERS - 1, coarse_sweep, solution)
    for repeat in range(SWEEPS - 1):
        solution = solution + factor * (source - apply_local(solution, stretch))
    residual_field = source - apply_local(solution, stretch)
    correction = cycle_whole(restrict(residual_field), level_index + 1)
    solution = solution + prolong(correction)
    for repeat in range(SWEEPS):
        solution = solution + factor * (source - apply_local(solution, stretch))
    return solution


def reference(magnetic):
    along_x, along_y, along_z = magnetic[0], magnetic[1], magnetic[2]
    divergence = (along_x - jnp.roll(along_x, 1, 0)) + (along_y - jnp.roll(along_y, 1, 1)) + (along_z - jnp.roll(along_z, 1, 2))
    potential = cycle_whole(-divergence, 0)
    cleaned_x = along_x - (jnp.roll(potential, -1, 0) - potential)
    cleaned_y = along_y - (jnp.roll(potential, -1, 1) - potential)
    cleaned_z = along_z - (jnp.roll(potential, -1, 2) - potential)
    return jnp.stack([cleaned_x, cleaned_y, cleaned_z])
```

```python
import functools
import itertools

import jax
import jax.numpy as jnp
from jax import lax
from jax.experimental import pallas as pl
from jax.experimental.pallas import tpu as pltpu
from jax.sharding import PartitionSpec as P

SWEEPS = 3
COARSE_ITERS = 24
MESH = pl.DeviceIdType.MESH
F32 = jnp.float32
NEAR = [d for d in itertools.product((-1, 0, 1), repeat=3) if d != (0, 0, 0)]
WIDE = NEAR + [(dx, dy, dz) for dx in (-2, 2) for dy in (-1, 0, 1) for dz in (-1, 0, 1)]
COUNT_X, COUNT_Y, COUNT_Z = 8, 4, 8
PLANE = [(a, b) for a in range(COUNT_X) for b in range(COUNT_Y) if (a, b) != (0, 0)]
SEVENTH = 1.0 / 7.0


def lane_of(shape):
    return lax.broadcasted_iota(jnp.int32, shape, len(shape) - 1)


def row_of(shape):
    return lax.broadcasted_iota(jnp.int32, shape, len(shape) - 2)


def turned(value, shift, axis):
    shift = shift % value.shape[axis]
    return value if shift == 0 else pltpu.roll(value, shift, axis)


def mixed(center, low, high):
    rows, lanes = center.ndim - 2, center.ndim - 1
    total = center + low + high
    total = total + (turned(center, 1, rows) + turned(center, -1, rows))
    total = total + (turned(center, 1, lanes) + turned(center, -1, lanes))
    return total * SEVENTH


def sweep(target, current, source, low, high, step):
    def body(index, carry):
        at = low + index * step
        mean = mixed(
            current[pl.ds(at, step)], current[pl.ds(at - 1, step)], current[pl.ds(at + 1, step)]
        )
        target[pl.ds(at, step)] = mean + source[pl.ds(at, step)]
        return carry

    lax.fori_loop(0, (high - low) // step, body, 0)


def residual_pair(current, source, at):
    center = current[pl.ds(at, 2)]
    mean = mixed(center, current[pl.ds(at - 1, 2)], current[pl.ds(at + 1, 2)])
    value = mean + source[pl.ds(at, 2)] - center
    return value[0] + value[1]


def selected(value, matrix):
    high = value.astype(jnp.bfloat16)
    low = (value - high.astype(F32)).astype(jnp.bfloat16)
    return jnp.dot(high, matrix, preferred_element_type=F32) + jnp.dot(
        low, matrix, preferred_element_type=F32
    )


def halving(period):
    lane, row = lane_of((128, 128)), row_of((128, 128))
    return jnp.where(row // 2 == lane % period, 0.5, 0.0).astype(jnp.bfloat16)


def doubling(lanes, wrap):
    lane, row = lane_of((128, lanes)), row_of((128, lanes))
    origin = lane // 2
    if wrap:
        origin = origin + jnp.where(lane >= 96, 64, 0)
    return jnp.where(row == origin, 1.0, 0.0).astype(jnp.bfloat16)


def row_pairs(ref, count, rows):
    pieces = [
        ref[index, pl.ds(0, rows, stride=2), :] + ref[index, pl.ds(1, rows, stride=2), :]
        for index in range(count)
    ]
    return jnp.concatenate(pieces, axis=0)


def kernel(magnetic, cleaned, *scratch):
    (
        field, result, low_x, low_y, low_z, last_y, last_z,
        source0, first0, second0, packed0, sides0, pairs0, spread0,
        slabs1, packed1, sides1, source1, first1, second1, pairs1, spread1,
        packed2, blocks2, source2, first2, second2, pairs2, spread2,
        lines3, gathered3, source3, level3, pairs3,
        load_sem, store_sem,
        send_a, recv_a, send_b, recv_b, send_c, recv_c, send_d, recv_d, send_e, recv_e, send_f, recv_f,
    ) = scratch
    me = (lax.axis_index("gx"), lax.axis_index("gy"), lax.axis_index("gz"))
    counts = (COUNT_X, COUNT_Y, COUNT_Z)

    def at(offset):
        return tuple(lax.rem(m + o + c, c) for m, o, c in zip(me, offset, counts))

    def remote(source, target, sends, recvs, index, offset):
        return pltpu.make_async_remote_copy(
            src_ref=source, dst_ref=target, send_sem=sends.at[index], recv_sem=recvs.at[index],
            device_id=at(offset), device_id_type=MESH,
        )

    pending = []

    def launch(copies):
        for copy in copies:
            copy.start()
        pending.extend(copies)

    def arrive(copies):
        for copy in copies:
            copy.wait_recv()

    loads = [pltpu.make_async_copy(magnetic.at[c], field.at[c], load_sem.at[c]) for c in range(3)]
    for load in loads:
        load.start()
    barrier = pltpu.get_barrier_semaphore()
    for offset in NEAR:
        pl.semaphore_signal(barrier, inc=1, device_id=at(offset), device_id_type=MESH)
    for load in loads:
        load.wait()

    lane32 = lane_of((32, 128))
    row32 = row_of((32, 128))

    last_y[...] = field[1, pl.ds(31, 16, stride=32), :]
    column = jnp.zeros((32, 128), F32)
    for x in range(16):
        column = jnp.where(
            lane32 == x, turned(field[2, x * 32 : x * 32 + 32, :], x + 1, 1), column
        )
    last_z[...] = column
    pl.semaphore_wait(barrier, len(NEAR))
    round_a = [
        remote(field.at[0, pl.ds(480, 32)], low_x, send_a, recv_a, 0, (1, 0, 0)),
        remote(last_y, low_y, send_a, recv_a, 1, (0, 1, 0)),
        remote(last_z, low_z, send_a, recv_a, 2, (0, 0, 1)),
    ]
    launch(round_a)
    arrive(round_a)

    column = low_z[...]
    halves = []
    edge = (lane32 < 8) | (lane32 >= 120)
    for half in range(2):
        total = jnp.zeros((32, 128), F32)
        for slot in range(8):
            x = half * 8 + slot
            own_x = field[0, x * 32 : x * 32 + 32, :]
            below_x = low_x[...] if x == 0 else field[0, x * 32 - 32 : x * 32, :]
            own_y = field[1, x * 32 : x * 32 + 32, :]
            below_y = jnp.where(row32 == 0, low_y[x : x + 1, :], turned(own_y, 1, 0))
            own_z = field[2, x * 32 : x * 32 + 32, :]
            below_z = jnp.where(lane32 == 0, turned(column, -x, 1), turned(own_z, 1, 1))
            value = ((below_x - own_x) + (below_y - own_y) + (below_z - own_z)) * SEVENTH
            source0[6 + x, 8:40, 0:128] = value
            total = total + turned(jnp.where(edge, value, 0.0), slot * 16, 1)
        packed0[:, half * 128 : half * 128 + 128] = total

    rows_from = {-1: (24, 8), 0: (0, 32), 1: (0, 8)}
    rows_to = {-1: 0, 0: 8, 1: 40}
    planes_from = {-1: (10, 6), 0: (0, 16), 1: (0, 6)}
    planes_to = {-1: 0, 0: 6, 1: 22}
    lanes_from = {-1: (128, 128), 0: (0, 256), 1: (0, 128)}
    lanes_to = {-1: 0, 0: 128, 1: 384}
    round_b = []
    for index, (dx, dy, dz) in enumerate(NEAR):
        (row, rows), peer = rows_from[dy], (-dx, -dy, -dz)
        if dz == 0:
            plane, planes = planes_from[dx]
            origin = source0.at[pl.ds(6 + plane, planes), pl.ds(8 + row, rows), pl.ds(0, 128)]
            target = source0.at[pl.ds(planes_to[dx], planes), pl.ds(rows_to[dy], rows), pl.ds(0, 128)]
        else:
            lane, lanes = lanes_from[dx]
            origin = packed0.at[pl.ds(row, rows), pl.ds(lane, lanes)]
            target = sides0.at[(dz + 1) // 2, pl.ds(rows_to[dy], rows), pl.ds(lanes_to[dx], lanes)]
        round_b.append(remote(origin, target, send_b, recv_b, index, peer))
    launch(round_b)
    arrive(round_b)

    lane48 = lane_of((48, 128))
    for group in range(4):
        lanes = slice(group * 128, group * 128 + 128)
        joined = jnp.where((lane48 // 8) % 2 == 1, sides0[0, :, lanes], sides0[1, :, lanes])
        for slot in range(8):
            x = group * 8 + slot - 8
            if -6 <= x < 22:
                source0[6 + x, :, 128:256] = turned(joined, -16 * slot, 1)
    sweep(first0, source0, source0, 1, 27, 2)
    sweep(second0, first0, source0, 2, 26, 2)

    def restrict0(index, carry):
        pairs0[index] = residual_pair(second0, source0, 6 + 2 * index)[8:40, 0:128]
        return carry

    lax.fori_loop(0, 8, restrict0, 0)

    coarse = selected(row_pairs(pairs0, 8, 16), halving(64)).reshape(8, 16, 128)
    lane16 = lane_of((16, 128))
    for x in range(4):
        slabs1[1, x, 8:24, :] = jnp.where(lane16 < 64, coarse[x], coarse[x + 4])
    edge = ((lane16 >= 64) & (lane16 < 72)) | (lane16 >= 120)
    total = jnp.zeros((16, 128), F32)
    for x in range(8):
        total = total + turned(jnp.where(edge, coarse[x], 0.0), 16 * x + 8, 1)
    packed1[...] = total
    rows_from = {-1: (8, 8), 0: (0, 16), 1: (0, 8)}
    rows_to = {-1: 0, 0: 8, 1: 24}
    round_c = []
    for index, (dx, dy, dz) in enumerate(NEAR):
        (row, rows), peer = rows_from[dy], (-dx, -dy, -dz)
        if dz == 0:
            origin = slabs1.at[1, :, pl.ds(8 + row, rows), :]
            target = slabs1.at[dx + 1, :, pl.ds(rows_to[dy], rows), :]
        else:
            origin = packed1.at[pl.ds(row, rows), :]
            target = sides1.at[(dz + 1) // 2, dx + 1, pl.ds(rows_to[dy], rows), :]
        round_c.append(remote(origin, target, send_c, recv_c, index, peer))
    launch(round_c)
    arrive(round_c)
    for group in range(3):
        joined = jnp.where((lane32 // 8) % 2 == 0, sides1[0, group], sides1[1, group])
        for x in range(8):
            main = slabs1[group, x % 4]
            if x >= 4:
                main = turned(main, 64, 1)
            side = turned(joined, -(16 * x + 8), 1)
            source1[group * 8 + x] = jnp.where(lane32 < 64, main, side)
    sweep(first1, source1, source1, 1, 23, 2)
    sweep(second1, first1, source1, 2, 22, 4)
    for index in range(4):
        pairs1[index] = residual_pair(second1, source1, 8 + 2 * index)[8:24, :]

    coarse = selected(row_pairs(pairs1, 4, 8), halving(32)).reshape(4, 8, 128)
    group8 = lane_of((8, 128)) // 32
    for step in (-1, 0, 1):
        total = coarse[3]
        for x in range(3):
            total = jnp.where(group8 == (x + step) % 4, coarse[x], total)
        if step == 0:
            blocks2[1, 2, 8:16, :] = total
        else:
            packed2[(step + 1) // 2] = total
    round_d = []
    for index, (dx, dy, dz) in enumerate(WIDE):
        origin = blocks2.at[1, 2, pl.ds(8, 8), :] if dz == 0 else packed2.at[(dz + 1) // 2]
        target = blocks2.at[dz + 1, dx + 2, pl.ds(8 * dy + 8, 8), :]
        round_d.append(remote(origin, target, send_d, recv_d, index, (-dx, -dy, -dz)))
    launch(round_d)
    arrive(round_d)
    group24 = lane_of((24, 128)) // 32
    for block in range(5):
        for x in range(4):
            value = jnp.where(group24 == (x + 1) % 4, blocks2[2, block], blocks2[0, block])
            value = jnp.where(group24 == x, blocks2[1, block], value)
            source2[block * 4 + x] = turned(value, -32 * x, 1)
    sweep(first2, source2, source2, 1, 19, 6)
    sweep(second2, first2, source2, 2, 18, 4)
    for index in range(2):
        pairs2[index] = residual_pair(second2, source2, 8 + 2 * index)[8:16, :]

    lines3[0] = selected(row_pairs(pairs2, 2, 4), halving(16))
    round_e = [
        remote(lines3.at[0], lines3.at[z], send_e, recv_e, z - 1, (0, 0, -z)) for z in range(1, COUNT_Z)
    ]
    launch(round_e)
    arrive(round_e)
    group8 = lane_of((8, 128)) // 16
    line = lines3[0]
    for z in range(1, COUNT_Z):
        line = jnp.where(group8 == z, lines3[z], line)
    gathered3[0, 0] = line
    round_f = [
        remote(gathered3.at[0, 0], gathered3.at[a, b], send_f, recv_f, index, (-a, -b, 0))
        for index, (a, b) in enumerate(PLANE)
    ]
    launch(round_f)
    arrive(round_f)
    for a in range(COUNT_X):
        for b in range(COUNT_Y):
            for x in range(2):
                source3[2 * a + x, 4 * b : 4 * b + 4, :] = gathered3[a, b, 4 * x : 4 * x + 4, :]

    def mixed_whole(value):
        below = jnp.concatenate([value[-1:], value[:-1]], axis=0)
        above = jnp.concatenate([value[1:], value[:1]], axis=0)
        return mixed(value, below, above)

    right = source3[...]
    value = right
    for repeat in range(SWEEPS - 1):
        value = mixed_whole(value) + right
    rest = mixed_whole(value) + right - value
    level3[...] = value
    rest = rest.reshape(8, 2, 16, 128)
    pairs3[...] = rest[:, 0] + rest[:, 1]

    coarse = selected(row_pairs(pairs3, 8, 8), halving(64)).reshape(8, 8, 128)
    error = lax.fori_loop(
        0, COARSE_ITERS - 1, lambda index, current: mixed_whole(current) + coarse, coarse
    )

    straight, wrapped = doubling(256, False), doubling(128, True)
    spread = selected(error.reshape(64, 128), straight[:, 0:128]).reshape(8, 8, 128)
    for x in range(8):
        pairs3[x, pl.ds(0, 8, stride=2), :] = spread[x]
        pairs3[x, pl.ds(1, 8, stride=2), :] = spread[x]
    spread = jnp.broadcast_to(pairs3[...][:, None], (8, 2, 16, 128)).reshape(16, 16, 128)
    value = level3[...] + spread
    for repeat in range(SWEEPS):
        value = mixed_whole(value) + right

    near = jnp.concatenate([value[13:16], value[0:5]], axis=0)
    near = turned(near, 4, 1)
    spread = selected(near.reshape(128, 128), wrapped).reshape(8, 16, 128)
    for x in range(8):
        spread2[x, pl.ds(0, 12, stride=2), :] = spread[x, 0:12]
        spread2[x, pl.ds(1, 12, stride=2), :] = spread[x, 0:12]
    for x in range(8):
        for side in range(2):
            second2[2 + 2 * x + side] = second2[2 + 2 * x + side] + spread2[x]
    sweep(first2, second2, source2, 3, 17, 7)
    sweep(second2, first2, source2, 4, 16, 6)
    sweep(first2, second2, source2, 5, 15, 5)

    near = first2[5:15, 4:20, :]
    spread = selected(near.reshape(160, 128), wrapped).reshape(10, 16, 128)
    for x in range(10):
        spread1[x, pl.ds(0, 16, stride=2), :] = spread[x]
        spread1[x, pl.ds(1, 16, stride=2), :] = spread[x]
    for x in range(10):
        for side in range(2):
            second1[2 + 2 * x + side] = second1[2 + 2 * x + side] + spread1[x]
    sweep(first1, second1, source1, 3, 21, 3)
    sweep(second1, first1, source1, 4, 20, 4)
    sweep(first1, second1, source1, 5, 19, 2)

    near = first1[6:18, 4:28, :]
    spread = selected(near.reshape(288, 128), straight).reshape(12, 24, 256)
    for x in range(12):
        for half in range(2):
            lanes = slice(half * 128, half * 128 + 128)
            spread0[half, x, pl.ds(0, 24, stride=2), :] = spread[x, :, lanes]
            spread0[half, x, pl.ds(1, 24, stride=2), :] = spread[x, :, lanes]

    def correct0(index, carry):
        for half in range(2):
            lanes = slice(half * 128, half * 128 + 128)
            for side in range(2):
                x = 2 + 2 * index + side
                second0[x, :, lanes] = second0[x, :, lanes] + spread0[half, index]
        return carry

    lax.fori_loop(0, 12, correct0, 0)
    sweep(first0, second0, source0, 3, 25, 2)
    sweep(second0, first0, source0, 4, 24, 2)
    sweep(first0, second0, source0, 5, 23, 2)

    def finish(x, carry):
        whole = first0[6 + x]
        here = whole[8:40, 0:128]
        above_x = first0[7 + x, 8:40, 0:128]
        above_y = turned(whole[:, 0:128], -1, 0)[8:40]
        above_z = turned(whole[8:40], -1, 1)[:, 0:128]
        rows = pl.ds(pl.multiple_of(x * 32, 32), 32)
        result[0, rows, :] = field[0, rows, :] - (above_x - here)
        result[1, rows, :] = field[1, rows, :] - (above_y - here)
        result[2, rows, :] = field[2, rows, :] - (above_z - here)
        return carry

    lax.fori_loop(0, 16, finish, 0)
    stores = [pltpu.make_async_copy(result.at[c], cleaned.at[c], store_sem.at[c]) for c in range(3)]
    for store in stores:
        store.start()
    for copy in pending:
        copy.wait_send()
    for store in stores:
        store.wait()


def scratch_shapes():
    def vmem(*shape):
        return pltpu.VMEM(shape, F32)

    dma = pltpu.SemaphoreType.DMA
    return [
        vmem(3, 512, 128), vmem(3, 512, 128), vmem(32, 128), vmem(16, 128), vmem(32, 128), vmem(16, 128), vmem(32, 128),
        vmem(28, 48, 256), vmem(28, 48, 256), vmem(28, 48, 256), vmem(32, 256), vmem(2, 48, 512), vmem(8, 32, 128), vmem(2, 12, 48, 128),
        vmem(3, 4, 32, 128), vmem(16, 128), vmem(2, 3, 32, 128), vmem(24, 32, 128), vmem(24, 32, 128), vmem(24, 32, 128), vmem(4, 16, 128), vmem(10, 32, 128),
        vmem(2, 8, 128), vmem(3, 5, 24, 128), vmem(20, 24, 128), vmem(20, 24, 128), vmem(20, 24, 128), vmem(2, 8, 128), vmem(8, 24, 128),
        vmem(8, 8, 128), vmem(8, 4, 8, 128), vmem(16, 16, 128), vmem(16, 16, 128), vmem(8, 16, 128),
        dma((3,)), dma((3,)),
        dma((3,)), dma((3,)), dma((26,)), dma((26,)), dma((26,)), dma((26,)), dma((44,)), dma((44,)), dma((7,)), dma((7,)), dma((31,)), dma((31,)),
    ]


def body(magnetic):
    cleaned = pl.pallas_call(
        kernel,
        out_shape=jax.ShapeDtypeStruct((3, 512, 128), F32),
        in_specs=[pl.BlockSpec(memory_space=pl.ANY)],
        out_specs=pl.BlockSpec(memory_space=pl.ANY),
        scratch_shapes=scratch_shapes(),
        compiler_params=pltpu.CompilerParams(
            collective_id=0, has_side_effects=True, vmem_limit_bytes=32 << 20
        ),
    )(magnetic.reshape(3, 512, 128))
    return cleaned.reshape(3, 16, 32, 128)


def solution(mesh):
    spec = P(None, "gx", "gy", "gz")
    return jax.shard_map(body, mesh=mesh, in_specs=(spec,), out_specs=spec, check_vma=False)
```

```python
import itertools

import jax
import jax.numpy as jnp
from jax import lax
from jax.experimental import pallas as pl
from jax.experimental.pallas import tpu as pltpu
from jax.sharding import PartitionSpec as P

SWEEPS = 3
COARSE_ITERS = 24
MESH = pl.DeviceIdType.MESH
F32 = jnp.float32
COUNT_X, COUNT_Y, COUNT_Z = 8, 4, 8
NEAR = sorted(
    (d for d in itertools.product((-1, 0, 1), repeat=3) if d != (0, 0, 0)),
    key=lambda d: -sum(map(abs, d)),
)
BULKY = sorted(NEAR, key=lambda d: d not in [(0, 1, 0), (0, -1, 0), (1, 0, 0), (-1, 0, 0)])
WIDE = [(dx, dy, dz) for dx in (-2, 2) for dy in (-1, 0, 1) for dz in (-1, 0, 1)]
LINE = sorted(range(1, COUNT_Z), key=lambda z: -min(z, COUNT_Z - z))
PLANE = sorted(
    ((a, b) for a in range(COUNT_X) for b in range(COUNT_Y) if (a, b) != (0, 0)),
    key=lambda d: -min(d[0], COUNT_X - d[0]) - 2 * min(d[1], COUNT_Y - d[1]),
)
SEVENTH = 1.0 / 7.0


def lane_of(shape):
    return lax.broadcasted_iota(jnp.int32, shape, len(shape) - 1)


def row_of(shape):
    return lax.broadcasted_iota(jnp.int32, shape, len(shape) - 2)


def turned(value, shift, axis):
    shift = shift % value.shape[axis]
    return value if shift == 0 else pltpu.roll(value, shift, axis)


def mixed(center, low, high):
    rows, lanes = center.ndim - 2, center.ndim - 1
    total = center + low + high
    total = total + (turned(center, 1, rows) + turned(center, -1, rows))
    total = total + (turned(center, 1, lanes) + turned(center, -1, lanes))
    return total * SEVENTH


def sweep(target, current, source, low, high, step):
    def body(index, carry):
        at = low + index * step
        mean = mixed(
            current[pl.ds(at, step)], current[pl.ds(at - 1, step)], current[pl.ds(at + 1, step)]
        )
        target[pl.ds(at, step)] = mean + source[pl.ds(at, step)]
        return carry

    lax.fori_loop(0, (high - low) // step, body, 0, unroll=True)


def residual_pair(current, source, at):
    center = current[pl.ds(at, 2)]
    mean = mixed(center, current[pl.ds(at - 1, 2)], current[pl.ds(at + 1, 2)])
    value = mean + source[pl.ds(at, 2)] - center
    return value[0] + value[1]


def selected(value, matrix):
    total = None
    for term in range(3):
        part = value.astype(jnp.bfloat16)
        value = value - part.astype(F32)
        product = jnp.dot(part, matrix, preferred_element_type=F32)
        total = product if total is None else total + product
    return total


def halving(period):
    lane, row = lane_of((128, 128)), row_of((128, 128))
    return jnp.where(row // 2 == lane % period, 0.5, 0.0).astype(jnp.bfloat16)


def doubling(lanes, wrap):
    lane, row = lane_of((128, lanes)), row_of((128, lanes))
    origin = lane // 2
    if wrap:
        origin = origin + jnp.where(lane >= 96, 64, 0)
    return jnp.where(row == origin, 1.0, 0.0).astype(jnp.bfloat16)


def row_pairs(ref, count, rows):
    pieces = [
        ref[index, pl.ds(0, rows, stride=2), :] + ref[index, pl.ds(1, rows, stride=2), :]
        for index in range(count)
    ]
    return jnp.concatenate(pieces, axis=0)


def kernel(field, result, *scratch):
    (
        low_x, low_y, low_z, last_y, last_z,
        source0, first0, second0, packed0, sides0, pairs0, spread0,
        slabs1, packed1, sides1, source1, first1, second1, pairs1, spread1,
        packed2, blocks2, source2, first2, second2, pairs2, spread2,
        lines3, gathered3, source3, level3, pairs3,
        halve0, halve1, halve2, straight, wrapped,
        send_a, recv_a, send_b, recv_b, send_c, recv_c, send_d, recv_d, send_e, recv_e, send_f, recv_f,
    ) = scratch
    me = (lax.axis_index("gx"), lax.axis_index("gy"), lax.axis_index("gz"))
    counts = (COUNT_X, COUNT_Y, COUNT_Z)

    def at(offset):
        return tuple(lax.rem(m + o + c, c) for m, o, c in zip(me, offset, counts))

    def remote(source, target, sends, recvs, index, offset):
        return pltpu.make_async_remote_copy(
            src_ref=source, dst_ref=target, send_sem=sends.at[index], recv_sem=recvs.at[index],
            device_id=at(offset), device_id_type=MESH,
        )

    def launch(copies):
        for copy in copies:
            copy.start()

    def sent(copies):
        for copy in copies:
            copy.wait_send()

    def arrive(copies):
        for copy in copies:
            copy.wait_recv()

    barrier = pltpu.get_barrier_semaphore()
    for offset in NEAR:
        pl.semaphore_signal(barrier, inc=1, device_id=at(offset), device_id_type=MESH)

    lane32 = lane_of((32, 128))
    row32 = row_of((32, 128))

    last_y[...] = field[1, pl.ds(31, 16, stride=32), :]
    column = jnp.zeros((32, 128), F32)
    for x in range(16):
        column = jnp.where(
            lane32 == x, turned(field[2, x * 32 : x * 32 + 32, :], x + 1, 1), column
        )
    last_z[...] = column
    pl.semaphore_wait(barrier, len(NEAR))
    round_a = [
        remote(field.at[0, pl.ds(480, 32)], low_x, send_a, recv_a, 0, (1, 0, 0)),
        remote(last_y, low_y, send_a, recv_a, 1, (0, 1, 0)),
        remote(last_z, low_z, send_a, recv_a, 2, (0, 0, 1)),
    ]
    launch(round_a)
    arrive(round_a)

    column = low_z[...]
    halves = []
    edge = (lane32 < 8) | (lane32 >= 120)
    for half in range(2):
        total = jnp.zeros((32, 128), F32)
        for slot in range(8):
            x = half * 8 + slot
            own_x = field[0, x * 32 : x * 32 + 32, :]
            below_x = low_x[...] if x == 0 else field[0, x * 32 - 32 : x * 32, :]
            own_y = field[1, x * 32 : x * 32 + 32, :]
            below_y = jnp.where(row32 == 0, low_y[x : x + 1, :], turned(own_y, 1, 0))
            own_z = field[2, x * 32 : x * 32 + 32, :]
            below_z = jnp.where(lane32 == 0, turned(column, -x, 1), turned(own_z, 1, 1))
            value = ((below_x - own_x) + (below_y - own_y) + (below_z - own_z)) * SEVENTH
            source0[6 + x, 8:40, 0:128] = value
            total = total + turned(jnp.where(edge, value, 0.0), slot * 16, 1)
        packed0[:, half * 128 : half * 128 + 128] = total

    rows_from = {-1: (24, 8), 0: (0, 32), 1: (0, 8)}
    rows_to = {-1: 0, 0: 8, 1: 40}
    planes_from = {-1: (10, 6), 0: (0, 16), 1: (0, 6)}
    planes_to = {-1: 0, 0: 6, 1: 22}
    lanes_from = {-1: (128, 128), 0: (0, 256), 1: (0, 128)}
    lanes_to = {-1: 0, 0: 128, 1: 384}
    round_b = []
    for index, (dx, dy, dz) in enumerate(BULKY):
        (row, rows), peer = rows_from[dy], (-dx, -dy, -dz)
        if dz == 0:
            plane, planes = planes_from[dx]
            origin = source0.at[pl.ds(6 + plane, planes), pl.ds(8 + row, rows), pl.ds(0, 128)]
            target = source0.at[pl.ds(planes_to[dx], planes), pl.ds(rows_to[dy], rows), pl.ds(0, 128)]
        else:
            lane, lanes = lanes_from[dx]
            origin = packed0.at[pl.ds(row, rows), pl.ds(lane, lanes)]
            target = sides0.at[(dz + 1) // 2, pl.ds(rows_to[dy], rows), pl.ds(lanes_to[dx], lanes)]
        round_b.append(remote(origin, target, send_b, recv_b, index, peer))
    launch(round_b)
    sent(round_a)
    halve0[...] = halving(64)
    halve1[...] = halving(32)
    halve2[...] = halving(16)
    straight[...] = doubling(256, False)
    wrapped[...] = doubling(128, True)
    arrive(round_b)

    lane48 = lane_of((48, 128))
    for group in range(4):
        lanes = slice(group * 128, group * 128 + 128)
        joined = jnp.where((lane48 // 8) % 2 == 1, sides0[0, :, lanes], sides0[1, :, lanes])
        for slot in range(8):
            x = group * 8 + slot - 8
            if -6 <= x < 22:
                source0[6 + x, :, 128:256] = turned(joined, -16 * slot, 1)
    sweep(first0, source0, source0, 4, 24, 2)
    sweep(second0, first0, source0, 5, 23, 2)

    def restrict0(index, carry):
        pairs0[index] = residual_pair(second0, source0, 6 + 2 * index)[8:40, 0:128]
        return carry

    lax.fori_loop(0, 8, restrict0, 0, unroll=True)

    coarse = selected(row_pairs(pairs0, 8, 16), halve0[...]).reshape(8, 16, 128)
    lane16 = lane_of((16, 128))
    for x in range(4):
        slabs1[1, x, 8:24, :] = jnp.where(lane16 < 64, coarse[x], coarse[x + 4])
    edge = ((lane16 >= 64) & (lane16 < 72)) | (lane16 >= 120)
    total = jnp.zeros((16, 128), F32)
    for x in range(8):
        total = total + turned(jnp.where(edge, coarse[x], 0.0), 16 * x + 8, 1)
    packed1[...] = total
    rows_from = {-1: (8, 8), 0: (0, 16), 1: (0, 8)}
    rows_to = {-1: 0, 0: 8, 1: 24}
    round_c = []
    for index, (dx, dy, dz) in enumerate(NEAR):
        (row, rows), peer = rows_from[dy], (-dx, -dy, -dz)
        if dz == 0:
            origin = slabs1.at[1, :, pl.ds(8 + row, rows), :]
            target = slabs1.at[dx + 1, :, pl.ds(rows_to[dy], rows), :]
        else:
            origin = packed1.at[pl.ds(row, rows), :]
            target = sides1.at[(dz + 1) // 2, dx + 1, pl.ds(rows_to[dy], rows), :]
        round_c.append(remote(origin, target, send_c, recv_c, index, peer))
    launch(round_c)
    sent(round_b)
    sweep(first0, source0, source0, 1, 4, 3)
    sweep(first0, source0, source0, 24, 27, 3)
    sweep(second0, first0, source0, 2, 5, 3)
    sweep(second0, first0, source0, 23, 26, 3)
    arrive(round_c)
    for group in range(3):
        joined = jnp.where((lane32 // 8) % 2 == 0, sides1[0, group], sides1[1, group])
        for x in range(8):
            main = slabs1[group, x % 4]
            if x >= 4:
                main = turned(main, 64, 1)
            side = turned(joined, -(16 * x + 8), 1)
            source1[group * 8 + x] = jnp.where(lane32 < 64, main, side)
    sweep(first1, source1, source1, 6, 18, 4)
    sweep(second1, first1, source1, 7, 17, 5)
    for index in range(4):
        pairs1[index] = residual_pair(second1, source1, 8 + 2 * index)[8:24, :]

    coarse = selected(row_pairs(pairs1, 4, 8), halve1[...]).reshape(4, 8, 128)
    group8 = lane_of((8, 128)) // 32
    for step in (-1, 0, 1):
        total = coarse[3]
        for x in range(3):
            total = jnp.where(group8 == (x + step) % 4, coarse[x], total)
        if step == 0:
            blocks2[1, 2, 8:16, :] = total
        else:
            packed2[(step + 1) // 2] = total
    round_d = []
    for index, (dx, dy, dz) in enumerate(NEAR + WIDE):
        origin = blocks2.at[1, 2, pl.ds(8, 8), :] if dz == 0 else packed2.at[(dz + 1) // 2]
        target = blocks2.at[dz + 1, dx + 2, pl.ds(8 * dy + 8, 8), :]
        round_d.append(remote(origin, target, send_d, recv_d, index, (-dx, -dy, -dz)))
    launch(round_d)
    sent(round_c)
    sweep(first1, source1, source1, 1, 6, 5)
    sweep(first1, source1, source1, 18, 23, 5)
    sweep(second1, first1, source1, 2, 7, 5)
    sweep(second1, first1, source1, 17, 22, 5)
    arrive(round_d[: len(NEAR)])
    group24 = lane_of((24, 128)) // 32

    def unpack2(block):
        for x in range(4):
            value = jnp.where(group24 == (x + 1) % 4, blocks2[2, block], blocks2[0, block])
            value = jnp.where(group24 == x, blocks2[1, block], value)
            source2[block * 4 + x] = turned(value, -32 * x, 1)

    for block in (1, 2, 3):
        unpack2(block)
    sweep(first2, source2, source2, 6, 14, 4)
    sweep(second2, first2, source2, 7, 13, 6)
    for index in range(2):
        pairs2[index] = residual_pair(second2, source2, 8 + 2 * index)[8:16, :]

    lines3[0] = selected(row_pairs(pairs2, 2, 4), halve2[...])
    round_e = [
        remote(lines3.at[0], lines3.at[z], send_e, recv_e, z - 1, (0, 0, -z)) for z in LINE
    ]
    launch(round_e)
    sent(round_d)
    arrive(round_d[len(NEAR) :])
    unpack2(0)
    unpack2(4)
    sweep(first2, source2, source2, 1, 6, 5)
    sweep(first2, source2, source2, 14, 19, 5)
    sweep(second2, first2, source2, 2, 7, 5)
    sweep(second2, first2, source2, 13, 18, 5)
    arrive(round_e)
    group8 = lane_of((8, 128)) // 16
    line = lines3[0]
    for z in range(1, COUNT_Z):
        line = jnp.where(group8 == z, lines3[z], line)
    gathered3[0, 0] = line
    round_f = [
        remote(gathered3.at[0, 0], gathered3.at[a, b], send_f, recv_f, index, (-a, -b, 0))
        for index, (a, b) in enumerate(PLANE)
    ]
    launch(round_f)
    sent(round_e)
    arrive(round_f)
    for a in range(COUNT_X):
        for b in range(COUNT_Y):
            for x in range(2):
                source3[2 * a + x, 4 * b : 4 * b + 4, :] = gathered3[a, b, 4 * x : 4 * x + 4, :]

    def mixed_whole(value):
        below = jnp.concatenate([value[-1:], value[:-1]], axis=0)
        above = jnp.concatenate([value[1:], value[:1]], axis=0)
        return mixed(value, below, above)

    right = source3[...]
    value = right
    for repeat in range(SWEEPS - 1):
        value = mixed_whole(value) + right
    rest = mixed_whole(value) + right - value
    level3[...] = value
    rest = rest.reshape(8, 2, 16, 128)
    pairs3[...] = rest[:, 0] + rest[:, 1]

    coarse = selected(row_pairs(pairs3, 8, 8), halve0[...]).reshape(8, 8, 128)
    error = lax.fori_loop(
        0, COARSE_ITERS - 1, lambda index, current: mixed_whole(current) + coarse, coarse
    )

    spread = selected(error.reshape(64, 128), straight[:, 0:128]).reshape(8, 8, 128)
    for x in range(8):
        pairs3[x, pl.ds(0, 8, stride=2), :] = spread[x]
        pairs3[x, pl.ds(1, 8, stride=2), :] = spread[x]
    spread = jnp.broadcast_to(pairs3[...][:, None], (8, 2, 16, 128)).reshape(16, 16, 128)
    value = level3[...] + spread
    for repeat in range(SWEEPS):
        value = mixed_whole(value) + right

    near = jnp.concatenate([value[13:16], value[0:5]], axis=0)
    near = turned(near, 4, 1)
    spread = selected(near.reshape(128, 128), wrapped[...]).reshape(8, 16, 128)
    for x in range(8):
        spread2[x, pl.ds(0, 12, stride=2), :] = spread[x, 0:12]
        spread2[x, pl.ds(1, 12, stride=2), :] = spread[x, 0:12]
    for x in range(8):
        for side in range(2):
            second2[2 + 2 * x + side] = second2[2 + 2 * x + side] + spread2[x]
    sweep(first2, second2, source2, 3, 17, 7)
    sweep(second2, first2, source2, 4, 16, 6)
    sweep(first2, second2, source2, 5, 15, 5)

    near = first2[5:15, 4:20, :]
    spread = selected(near.reshape(160, 128), wrapped[...]).reshape(10, 16, 128)
    for x in range(10):
        spread1[x, pl.ds(0, 16, stride=2), :] = spread[x]
        spread1[x, pl.ds(1, 16, stride=2), :] = spread[x]
    for x in range(10):
        for side in range(2):
            second1[2 + 2 * x + side] = second1[2 + 2 * x + side] + spread1[x]
    sweep(first1, second1, source1, 3, 21, 3)
    sweep(second1, first1, source1, 4, 20, 4)
    sweep(first1, second1, source1, 5, 19, 2)

    near = first1[6:18, 4:28, :]
    spread = selected(near.reshape(288, 128), straight[...]).reshape(12, 24, 256)
    for x in range(12):
        for half in range(2):
            lanes = slice(half * 128, half * 128 + 128)
            spread0[half, x, pl.ds(0, 24, stride=2), :] = spread[x, :, lanes]
            spread0[half, x, pl.ds(1, 24, stride=2), :] = spread[x, :, lanes]

    def correct0(index, carry):
        for half in range(2):
            lanes = slice(half * 128, half * 128 + 128)
            for side in range(2):
                x = 2 + 2 * index + side
                second0[x, :, lanes] = second0[x, :, lanes] + spread0[half, index]
        return carry

    lax.fori_loop(0, 12, correct0, 0, unroll=True)
    sweep(first0, second0, source0, 3, 25, 2)
    sweep(second0, first0, source0, 4, 24, 2)
    sweep(first0, second0, source0, 5, 23, 2)

    def finish(x, carry):
        whole = first0[6 + x]
        here = whole[8:40, 0:128]
        above_x = first0[7 + x, 8:40, 0:128]
        above_y = turned(whole[:, 0:128], -1, 0)[8:40]
        above_z = turned(whole[8:40], -1, 1)[:, 0:128]
        rows = pl.ds(pl.multiple_of(x * 32, 32), 32)
        result[0, rows, :] = field[0, rows, :] - (above_x - here)
        result[1, rows, :] = field[1, rows, :] - (above_y - here)
        result[2, rows, :] = field[2, rows, :] - (above_z - here)
        return carry

    lax.fori_loop(0, 16, finish, 0, unroll=True)
    sent(round_f)


def scratch_shapes():
    def vmem(*shape):
        return pltpu.VMEM(shape, F32)

    def half(lanes):
        return pltpu.VMEM((128, lanes), jnp.bfloat16)

    dma = pltpu.SemaphoreType.DMA
    return [
        vmem(32, 128), vmem(16, 128), vmem(32, 128), vmem(16, 128), vmem(32, 128),
        vmem(28, 48, 256), vmem(28, 48, 256), vmem(28, 48, 256), vmem(32, 256), vmem(2, 48, 512), vmem(8, 32, 128), vmem(2, 12, 48, 128),
        vmem(3, 4, 32, 128), vmem(16, 128), vmem(2, 3, 32, 128), vmem(24, 32, 128), vmem(24, 32, 128), vmem(24, 32, 128), vmem(4, 16, 128), vmem(10, 32, 128),
        vmem(2, 8, 128), vmem(3, 5, 24, 128), vmem(20, 24, 128), vmem(20, 24, 128), vmem(20, 24, 128), vmem(2, 8, 128), vmem(8, 24, 128),
        vmem(8, 8, 128), vmem(8, 4, 8, 128), vmem(16, 16, 128), vmem(16, 16, 128), vmem(8, 16, 128),
        half(128), half(128), half(128), half(256), half(128),
        dma((3,)), dma((3,)), dma((26,)), dma((26,)), dma((26,)), dma((26,)), dma((44,)), dma((44,)), dma((7,)), dma((7,)), dma((31,)), dma((31,)),
    ]


def body(magnetic):
    cleaned = pl.pallas_call(
        kernel,
        out_shape=jax.ShapeDtypeStruct((3, 512, 128), F32),
        in_specs=[pl.BlockSpec(memory_space=pltpu.VMEM)],
        out_specs=pl.BlockSpec(memory_space=pltpu.VMEM),
        scratch_shapes=scratch_shapes(),
        compiler_params=pltpu.CompilerParams(
            collective_id=0, has_side_effects=True, vmem_limit_bytes=32 << 20
        ),
    )(magnetic.reshape(3, 512, 128))
    return cleaned.reshape(3, 16, 32, 128)


def solution(mesh):
    spec = P(None, "gx", "gy", "gz")
    return jax.shard_map(body, mesh=mesh, in_specs=(spec,), out_specs=spec, check_vma=False)
```

```python
import itertools

import jax
import jax.numpy as jnp
from jax import lax
from jax.experimental import pallas as pl
from jax.experimental.pallas import tpu as pltpu
from jax.sharding import PartitionSpec as P

SWEEPS = 3
COARSE_ITERS = 24
MESH = pl.DeviceIdType.MESH
F32 = jnp.float32
COUNT_X, COUNT_Y, COUNT_Z = 8, 4, 8
NEAR = sorted(
    (d for d in itertools.product((-1, 0, 1), repeat=3) if d != (0, 0, 0)),
    key=lambda d: -sum(map(abs, d)),
)
GREETED = [d for d in NEAR if sum(map(abs, d)) != 2]
BULKY = sorted(NEAR, key=lambda d: d not in [(0, 1, 0), (0, -1, 0), (1, 0, 0), (-1, 0, 0)])
WIDE = [(dx, dy, dz) for dx in (-2, 2) for dy in (-1, 0, 1) for dz in (-1, 0, 1)]
LINE = sorted(range(1, COUNT_Z), key=lambda z: -min(z, COUNT_Z - z))
PLANE = sorted(
    ((a, b) for a in range(COUNT_X) for b in range(COUNT_Y) if (a, b) != (0, 0)),
    key=lambda d: -min(d[0], COUNT_X - d[0]) - 2 * min(d[1], COUNT_Y - d[1]),
)
SEVENTH = 1.0 / 7.0


def lane_of(shape):
    return lax.broadcasted_iota(jnp.int32, shape, len(shape) - 1)


def row_of(shape):
    return lax.broadcasted_iota(jnp.int32, shape, len(shape) - 2)


def turned(value, shift, axis):
    shift = shift % value.shape[axis]
    return value if shift == 0 else pltpu.roll(value, shift, axis)


def mixed(center, low, high):
    rows, lanes = center.ndim - 2, center.ndim - 1
    total = center + low + high
    total = total + (turned(center, 1, rows) + turned(center, -1, rows))
    total = total + (turned(center, 1, lanes) + turned(center, -1, lanes))
    return total * SEVENTH


def sweep(target, current, source, low, high, step):
    def body(index, carry):
        at = low + index * step
        mean = mixed(
            current[pl.ds(at, step)], current[pl.ds(at - 1, step)], current[pl.ds(at + 1, step)]
        )
        target[pl.ds(at, step)] = mean + source[pl.ds(at, step)]
        return carry

    lax.fori_loop(0, (high - low) // step, body, 0, unroll=True)


def residual_pair(current, source, at):
    center = current[pl.ds(at, 2)]
    mean = mixed(center, current[pl.ds(at - 1, 2)], current[pl.ds(at + 1, 2)])
    value = mean + source[pl.ds(at, 2)] - center
    return value[0] + value[1]


def selected(value, matrix):
    total = None
    for term in range(3):
        part = value.astype(jnp.bfloat16)
        value = value - part.astype(F32)
        product = jnp.dot(part, matrix, preferred_element_type=F32)
        total = product if total is None else total + product
    return total


def halving(period):
    lane, row = lane_of((128, 128)), row_of((128, 128))
    return jnp.where(row // 2 == lane % period, 0.5, 0.0).astype(jnp.bfloat16)


def doubling(lanes, wrap):
    lane, row = lane_of((128, lanes)), row_of((128, lanes))
    origin = lane // 2
    if wrap:
        origin = origin + jnp.where(lane >= 96, 64, 0)
    return jnp.where(row == origin, 1.0, 0.0).astype(jnp.bfloat16)


def row_pairs(ref, count, rows):
    pieces = [
        ref[index, pl.ds(0, rows, stride=2), :] + ref[index, pl.ds(1, rows, stride=2), :]
        for index in range(count)
    ]
    return jnp.concatenate(pieces, axis=0)


def kernel(magnetic, result, *scratch):
    (
        field, low_x, low_y, low_z, last_y, last_z,
        source0, first0, second0, packed0, sides0, pairs0, spread0,
        slabs1, packed1, sides1, source1, first1, second1, pairs1, spread1,
        packed2, blocks2, source2, first2, second2, pairs2, spread2,
        lines3, gathered3, source3, level3, pairs3,
        halve0, halve1, halve2, straight, wrapped,
        load_sem, enter_sem,
        send_a, recv_a, send_b, recv_b, send_c, recv_c, send_d, recv_d, send_e, recv_e, send_f, recv_f,
    ) = scratch
    me = (lax.axis_index("gx"), lax.axis_index("gy"), lax.axis_index("gz"))
    counts = (COUNT_X, COUNT_Y, COUNT_Z)

    def at(offset):
        return tuple(lax.rem(m + o + c, c) for m, o, c in zip(me, offset, counts))

    def remote(source, target, sends, recvs, index, offset):
        return pltpu.make_async_remote_copy(
            src_ref=source, dst_ref=target, send_sem=sends.at[index], recv_sem=recvs.at[index],
            device_id=at(offset), device_id_type=MESH,
        )

    def launch(copies):
        for copy in copies:
            copy.start()

    def sent(copies):
        for copy in copies:
            copy.wait_send()

    def arrive(copies):
        for copy in copies:
            copy.wait_recv()

    loads = [pltpu.make_async_copy(magnetic.at[c], field.at[c], load_sem.at[c]) for c in range(3)]
    for load in loads:
        load.start()
    barrier = pltpu.get_barrier_semaphore()
    for offset in GREETED:
        pl.semaphore_signal(barrier, inc=1, device_id=at(offset), device_id_type=MESH)
    for load in loads:
        load.wait()

    lane32 = lane_of((32, 128))
    row32 = row_of((32, 128))

    last_y[...] = field[1, pl.ds(31, 16, stride=32), :]
    column = jnp.zeros((32, 128), F32)
    for x in range(16):
        column = jnp.where(
            lane32 == x, turned(field[2, x * 32 : x * 32 + 32, :], x + 1, 1), column
        )
    last_z[...] = column
    pl.semaphore_wait(barrier, len(GREETED))
    round_a = [
        remote(field.at[0, pl.ds(480, 32)], low_x, send_a, recv_a, 0, (1, 0, 0)),
        remote(last_y, low_y, send_a, recv_a, 1, (0, 1, 0)),
        remote(last_z, low_z, send_a, recv_a, 2, (0, 0, 1)),
    ]
    launch(round_a)
    for offset in ((-1, 0, 0), (0, -1, 0), (0, 0, -1)):
        pl.semaphore_signal(enter_sem, inc=1, device_id=at(offset), device_id_type=MESH)
    pl.semaphore_wait(enter_sem, 3)
    arrive(round_a)

    column = low_z[...]
    halves = []
    edge = (lane32 < 8) | (lane32 >= 120)
    for half in range(2):
        total = jnp.zeros((32, 128), F32)
        for slot in range(8):
            x = half * 8 + slot
            own_x = field[0, x * 32 : x * 32 + 32, :]
            below_x = low_x[...] if x == 0 else field[0, x * 32 - 32 : x * 32, :]
            own_y = field[1, x * 32 : x * 32 + 32, :]
            below_y = jnp.where(row32 == 0, low_y[x : x + 1, :], turned(own_y, 1, 0))
            own_z = field[2, x * 32 : x * 32 + 32, :]
            below_z = jnp.where(lane32 == 0, turned(column, -x, 1), turned(own_z, 1, 1))
            value = ((below_x - own_x) + (below_y - own_y) + (below_z - own_z)) * SEVENTH
            source0[6 + x, 8:40, 0:128] = value
            total = total + turned(jnp.where(edge, value, 0.0), slot * 16, 1)
        packed0[:, half * 128 : half * 128 + 128] = total

    rows_from = {-1: (24, 8), 0: (0, 32), 1: (0, 8)}
    rows_to = {-1: 0, 0: 8, 1: 40}
    planes_from = {-1: (10, 6), 0: (0, 16), 1: (0, 6)}
    planes_to = {-1: 0, 0: 6, 1: 22}
    lanes_from = {-1: (128, 128), 0: (0, 256), 1: (0, 128)}
    lanes_to = {-1: 0, 0: 128, 1: 384}
    round_b = []
    for index, (dx, dy, dz) in enumerate(BULKY):
        (row, rows), peer = rows_from[dy], (-dx, -dy, -dz)
        if dz == 0:
            plane, planes = planes_from[dx]
            origin = source0.at[pl.ds(6 + plane, planes), pl.ds(8 + row, rows), pl.ds(0, 128)]
            target = source0.at[pl.ds(planes_to[dx], planes), pl.ds(rows_to[dy], rows), pl.ds(0, 128)]
        else:
            lane, lanes = lanes_from[dx]
            origin = packed0.at[pl.ds(row, rows), pl.ds(lane, lanes)]
            target = sides0.at[(dz + 1) // 2, pl.ds(rows_to[dy], rows), pl.ds(lanes_to[dx], lanes)]
        round_b.append(remote(origin, target, send_b, recv_b, index, peer))
    launch(round_b)
    sent(round_a)
    halve0[...] = halving(64)
    halve1[...] = halving(32)
    halve2[...] = halving(16)
    straight[...] = doubling(256, False)
    wrapped[...] = doubling(128, True)
    arrive(round_b)

    lane48 = lane_of((48, 128))
    for group in range(4):
        lanes = slice(group * 128, group * 128 + 128)
        joined = jnp.where((lane48 // 8) % 2 == 1, sides0[0, :, lanes], sides0[1, :, lanes])
        for slot in range(8):
            x = group * 8 + slot - 8
            if -6 <= x < 22:
                source0[6 + x, :, 128:256] = turned(joined, -16 * slot, 1)
    sweep(first0, source0, source0, 4, 24, 2)
    sweep(second0, first0, source0, 5, 23, 2)

    def restrict0(index, carry):
        pairs0[index] = residual_pair(second0, source0, 6 + 2 * index)[8:40, 0:128]
        return carry

    lax.fori_loop(0, 8, restrict0, 0, unroll=True)

    coarse = selected(row_pairs(pairs0, 8, 16), halve0[...]).reshape(8, 16, 128)
    lane16 = lane_of((16, 128))
    for x in range(4):
        slabs1[1, x, 8:24, :] = jnp.where(lane16 < 64, coarse[x], coarse[x + 4])
    edge = ((lane16 >= 64) & (lane16 < 72)) | (lane16 >= 120)
    total = jnp.zeros((16, 128), F32)
    for x in range(8):
        total = total + turned(jnp.where(edge, coarse[x], 0.0), 16 * x + 8, 1)
    packed1[...] = total
    rows_from = {-1: (8, 8), 0: (0, 16), 1: (0, 8)}
    rows_to = {-1: 0, 0: 8, 1: 24}
    round_c = []
    for index, (dx, dy, dz) in enumerate(NEAR):
        (row, rows), peer = rows_from[dy], (-dx, -dy, -dz)
        if dz == 0:
            origin = slabs1.at[1, :, pl.ds(8 + row, rows), :]
            target = slabs1.at[dx + 1, :, pl.ds(rows_to[dy], rows), :]
        else:
            origin = packed1.at[pl.ds(row, rows), :]
            target = sides1.at[(dz + 1) // 2, dx + 1, pl.ds(rows_to[dy], rows), :]
        round_c.append(remote(origin, target, send_c, recv_c, index, peer))
    launch(round_c)
    sent(round_b)
    sweep(first0, source0, source0, 1, 4, 3)
    sweep(first0, source0, source0, 24, 27, 3)
    sweep(second0, first0, source0, 2, 5, 3)
    sweep(second0, first0, source0, 23, 26, 3)
    arrive(round_c)
    for group in range(3):
        joined = jnp.where((lane32 // 8) % 2 == 0, sides1[0, group], sides1[1, group])
        for x in range(8):
            main = slabs1[group, x % 4]
            if x >= 4:
                main = turned(main, 64, 1)
            side = turned(joined, -(16 * x + 8), 1)
            source1[group * 8 + x] = jnp.where(lane32 < 64, main, side)
    sweep(first1, source1, source1, 6, 18, 4)
    sweep(second1, first1, source1, 7, 17, 5)
    for index in range(4):
        pairs1[index] = residual_pair(second1, source1, 8 + 2 * index)[8:24, :]

    coarse = selected(row_pairs(pairs1, 4, 8), halve1[...]).reshape(4, 8, 128)
    group8 = lane_of((8, 128)) // 32
    for step in (-1, 0, 1):
        total = coarse[3]
        for x in range(3):
            total = jnp.where(group8 == (x + step) % 4, coarse[x], total)
        if step == 0:
            blocks2[1, 2, 8:16, :] = total
        else:
            packed2[(step + 1) // 2] = total
    round_d = []
    for index, (dx, dy, dz) in enumerate(NEAR + WIDE):
        origin = blocks2.at[1, 2, pl.ds(8, 8), :] if dz == 0 else packed2.at[(dz + 1) // 2]
        target = blocks2.at[dz + 1, dx + 2, pl.ds(8 * dy + 8, 8), :]
        round_d.append(remote(origin, target, send_d, recv_d, index, (-dx, -dy, -dz)))
    launch(round_d)
    sent(round_c)
    sweep(first1, source1, source1, 1, 6, 5)
    sweep(first1, source1, source1, 18, 23, 5)
    sweep(second1, first1, source1, 2, 7, 5)
    sweep(second1, first1, source1, 17, 22, 5)
    arrive(round_d[: len(NEAR)])
    group24 = lane_of((24, 128)) // 32

    def unpack2(block):
        for x in range(4):
            value = jnp.where(group24 == (x + 1) % 4, blocks2[2, block], blocks2[0, block])
            value = jnp.where(group24 == x, blocks2[1, block], value)
            source2[block * 4 + x] = turned(value, -32 * x, 1)

    for block in (1, 2, 3):
        unpack2(block)
    sweep(first2, source2, source2, 6, 14, 4)
    sweep(second2, first2, source2, 7, 13, 6)
    for index in range(2):
        pairs2[index] = residual_pair(second2, source2, 8 + 2 * index)[8:16, :]

    lines3[0] = selected(row_pairs(pairs2, 2, 4), halve2[...])
    round_e = [
        remote(lines3.at[0], lines3.at[z], send_e, recv_e, z - 1, (0, 0, -z)) for z in LINE
    ]
    launch(round_e)
    sent(round_d)
    arrive(round_d[len(NEAR) :])
    unpack2(0)
    unpack2(4)
    sweep(first2, source2, source2, 1, 6, 5)
    sweep(first2, source2, source2, 14, 19, 5)
    sweep(second2, first2, source2, 2, 7, 5)
    sweep(second2, first2, source2, 13, 18, 5)
    arrive(round_e)
    group8 = lane_of((8, 128)) // 16
    line = lines3[0]
    for z in range(1, COUNT_Z):
        line = jnp.where(group8 == z, lines3[z], line)
    gathered3[0, 0] = line
    round_f = [
        remote(gathered3.at[0, 0], gathered3.at[a, b], send_f, recv_f, index, (-a, -b, 0))
        for index, (a, b) in enumerate(PLANE)
    ]
    launch(round_f)
    sent(round_e)
    arrive(round_f)
    for a in range(COUNT_X):
        for b in range(COUNT_Y):
            for x in range(2):
                source3[2 * a + x, 4 * b : 4 * b + 4, :] = gathered3[a, b, 4 * x : 4 * x + 4, :]

    def mixed_whole(value):
        below = jnp.concatenate([value[-1:], value[:-1]], axis=0)
        above = jnp.concatenate([value[1:], value[:1]], axis=0)
        return mixed(value, below, above)

    right = source3[...]
    value = right
    for repeat in range(SWEEPS - 1):
        value = mixed_whole(value) + right
    rest = mixed_whole(value) + right - value
    level3[...] = value
    rest = rest.reshape(8, 2, 16, 128)
    pairs3[...] = rest[:, 0] + rest[:, 1]

    coarse = selected(row_pairs(pairs3, 8, 8), halve0[...]).reshape(8, 8, 128)
    error = lax.fori_loop(
        0, COARSE_ITERS - 1, lambda index, current: mixed_whole(current) + coarse, coarse
    )

    spread = selected(error.reshape(64, 128), straight[:, 0:128]).reshape(8, 8, 128)
    for x in range(8):
        pairs3[x, pl.ds(0, 8, stride=2), :] = spread[x]
        pairs3[x, pl.ds(1, 8, stride=2), :] = spread[x]
    spread = jnp.broadcast_to(pairs3[...][:, None], (8, 2, 16, 128)).reshape(16, 16, 128)
    value = level3[...] + spread
    for repeat in range(SWEEPS):
        value = mixed_whole(value) + right

    near = jnp.concatenate([value[13:16], value[0:5]], axis=0)
    near = turned(near, 4, 1)
    spread = selected(near.reshape(128, 128), wrapped[...]).reshape(8, 16, 128)
    for x in range(8):
        spread2[x, pl.ds(0, 12, stride=2), :] = spread[x, 0:12]
        spread2[x, pl.ds(1, 12, stride=2), :] = spread[x, 0:12]
    for x in range(8):
        for side in range(2):
            second2[2 + 2 * x + side] = second2[2 + 2 * x + side] + spread2[x]
    sweep(first2, second2, source2, 3, 17, 7)
    sweep(second2, first2, source2, 4, 16, 6)
    sweep(first2, second2, source2, 5, 15, 5)

    near = first2[5:15, 4:20, :]
    spread = selected(near.reshape(160, 128), wrapped[...]).reshape(10, 16, 128)
    for x in range(10):
        spread1[x, pl.ds(0, 16, stride=2), :] = spread[x]
        spread1[x, pl.ds(1, 16, stride=2), :] = spread[x]
    for x in range(10):
        for side in range(2):
            second1[2 + 2 * x + side] = second1[2 + 2 * x + side] + spread1[x]
    sweep(first1, second1, source1, 3, 21, 3)
    sweep(second1, first1, source1, 4, 20, 4)
    sweep(first1, second1, source1, 5, 19, 2)

    near = first1[6:18, 4:28, :]
    spread = selected(near.reshape(288, 128), straight[...]).reshape(12, 24, 256)
    for x in range(12):
        for half in range(2):
            lanes = slice(half * 128, half * 128 + 128)
            spread0[half, x, pl.ds(0, 24, stride=2), :] = spread[x, :, lanes]
            spread0[half, x, pl.ds(1, 24, stride=2), :] = spread[x, :, lanes]

    def correct0(index, carry):
        for half in range(2):
            lanes = slice(half * 128, half * 128 + 128)
            for side in range(2):
                x = 2 + 2 * index + side
                second0[x, :, lanes] = second0[x, :, lanes] + spread0[half, index]
        return carry

    lax.fori_loop(0, 12, correct0, 0, unroll=True)
    sweep(first0, second0, source0, 3, 25, 2)
    sweep(second0, first0, source0, 4, 24, 2)
    sweep(first0, second0, source0, 5, 23, 2)

    def finish(x, carry):
        whole = first0[6 + x]
        here = whole[8:40, 0:128]
        above_x = first0[7 + x, 8:40, 0:128]
        above_y = turned(whole[:, 0:128], -1, 0)[8:40]
        above_z = turned(whole[8:40], -1, 1)[:, 0:128]
        rows = pl.ds(pl.multiple_of(x * 32, 32), 32)
        result[0, rows, :] = field[0, rows, :] - (above_x - here)
        result[1, rows, :] = field[1, rows, :] - (above_y - here)
        result[2, rows, :] = field[2, rows, :] - (above_z - here)
        return carry

    lax.fori_loop(0, 16, finish, 0, unroll=True)
    sent(round_f)


def scratch_shapes():
    def vmem(*shape):
        return pltpu.VMEM(shape, F32)

    def half(lanes):
        return pltpu.VMEM((128, lanes), jnp.bfloat16)

    dma = pltpu.SemaphoreType.DMA
    return [
        vmem(3, 512, 128), vmem(32, 128), vmem(16, 128), vmem(32, 128), vmem(16, 128), vmem(32, 128),
        vmem(28, 48, 256), vmem(28, 48, 256), vmem(28, 48, 256), vmem(32, 256), vmem(2, 48, 512), vmem(8, 32, 128), vmem(2, 12, 48, 128),
        vmem(3, 4, 32, 128), vmem(16, 128), vmem(2, 3, 32, 128), vmem(24, 32, 128), vmem(24, 32, 128), vmem(24, 32, 128), vmem(4, 16, 128), vmem(10, 32, 128),
        vmem(2, 8, 128), vmem(3, 5, 24, 128), vmem(20, 24, 128), vmem(20, 24, 128), vmem(20, 24, 128), vmem(2, 8, 128), vmem(8, 24, 128),
        vmem(8, 8, 128), vmem(8, 4, 8, 128), vmem(16, 16, 128), vmem(16, 16, 128), vmem(8, 16, 128),
        half(128), half(128), half(128), half(256), half(128),
        dma((3,)), pltpu.SemaphoreType.REGULAR,
        dma((3,)), dma((3,)), dma((26,)), dma((26,)), dma((26,)), dma((26,)), dma((44,)), dma((44,)), dma((7,)), dma((7,)), dma((31,)), dma((31,)),
    ]


def body(magnetic):
    cleaned = pl.pallas_call(
        kernel,
        out_shape=jax.ShapeDtypeStruct((3, 512, 128), F32),
        in_specs=[pl.BlockSpec(memory_space=pl.ANY)],
        out_specs=pl.BlockSpec(memory_space=pltpu.VMEM),
        scratch_shapes=scratch_shapes(),
        compiler_params=pltpu.CompilerParams(
            collective_id=0, has_side_effects=True, vmem_limit_bytes=53 << 20
        ),
    )(magnetic.reshape(3, 512, 128))
    return cleaned.reshape(3, 16, 32, 128)


def solution(mesh):
    spec = P(None, "gx", "gy", "gz")
    return jax.shard_map(body, mesh=mesh, in_specs=(spec,), out_specs=spec, check_vma=False)
```

```python
import itertools

import jax
import jax.numpy as jnp
from jax import lax
from jax.experimental import pallas as pl
from jax.experimental.pallas import tpu as pltpu
from jax.sharding import PartitionSpec as P

SWEEPS = 3
COARSE_ITERS = 24
MESH = pl.DeviceIdType.MESH
F32 = jnp.float32
COUNT_X, COUNT_Y, COUNT_Z = 8, 4, 8
NEAR = sorted(
    (d for d in itertools.product((-1, 0, 1), repeat=3) if d != (0, 0, 0)),
    key=lambda d: -sum(map(abs, d)),
)
GREETED = [d for d in NEAR if sum(map(abs, d)) != 2]
BULKY = sorted(NEAR, key=lambda d: d not in [(0, 1, 0), (0, -1, 0), (1, 0, 0), (-1, 0, 0)])
WIDE = [(dx, dy, dz) for dx in (-2, 2) for dy in (-1, 0, 1) for dz in (-1, 0, 1)]
LINE = sorted(range(1, COUNT_Z), key=lambda z: -min(z, COUNT_Z - z))
PLANE = sorted(
    ((a, b) for a in range(COUNT_X) for b in range(COUNT_Y) if (a, b) != (0, 0)),
    key=lambda d: -min(d[0], COUNT_X - d[0]) - 2 * min(d[1], COUNT_Y - d[1]),
)
SEVENTH = 1.0 / 7.0


def lane_of(shape):
    return lax.broadcasted_iota(jnp.int32, shape, len(shape) - 1)


def row_of(shape):
    return lax.broadcasted_iota(jnp.int32, shape, len(shape) - 2)


def turned(value, shift, axis):
    shift = shift % value.shape[axis]
    return value if shift == 0 else pltpu.roll(value, shift, axis)


def mixed(center, low, high):
    rows, lanes = center.ndim - 2, center.ndim - 1
    total = center + low + high
    total = total + (turned(center, 1, rows) + turned(center, -1, rows))
    total = total + (turned(center, 1, lanes) + turned(center, -1, lanes))
    return total * SEVENTH


def sweep(target, current, source, low, high, step):
    def body(index, carry):
        at = low + index * step
        mean = mixed(
            current[pl.ds(at, step)], current[pl.ds(at - 1, step)], current[pl.ds(at + 1, step)]
        )
        target[pl.ds(at, step)] = mean + source[pl.ds(at, step)]
        return carry

    lax.fori_loop(0, (high - low) // step, body, 0, unroll=True)


def residual_pair(current, source, at):
    center = current[pl.ds(at, 2)]
    mean = mixed(center, current[pl.ds(at - 1, 2)], current[pl.ds(at + 1, 2)])
    value = mean + source[pl.ds(at, 2)] - center
    return value[0] + value[1]


def selected(value, matrix):
    total = None
    for term in range(3):
        part = value.astype(jnp.bfloat16)
        value = value - part.astype(F32)
        product = jnp.dot(part, matrix, preferred_element_type=F32)
        total = product if total is None else total + product
    return total


def halving(period):
    lane, row = lane_of((128, 128)), row_of((128, 128))
    return jnp.where(row // 2 == lane % period, 0.5, 0.0).astype(jnp.bfloat16)


def doubling(lanes, wrap):
    lane, row = lane_of((128, lanes)), row_of((128, lanes))
    origin = lane // 2
    if wrap:
        origin = origin + jnp.where(lane >= 96, 64, 0)
    return jnp.where(row == origin, 1.0, 0.0).astype(jnp.bfloat16)


def row_pairs(ref, count, rows):
    pieces = [
        ref[index, pl.ds(0, rows, stride=2), :] + ref[index, pl.ds(1, rows, stride=2), :]
        for index in range(count)
    ]
    return jnp.concatenate(pieces, axis=0)


def kernel(magnetic, result, *scratch):
    (
        field, low_x, low_y, low_z, last_y, last_z,
        source0, first0, second0, packed0, sides0, pairs0, spread0,
        slabs1, packed1, sides1, source1, first1, second1, pairs1, spread1,
        packed2, blocks2, source2, first2, second2, pairs2, spread2,
        lines3, gathered3, source3, level3, pairs3,
        halve0, halve1, halve2, straight, wrapped,
        load_sem, enter_sem,
        send_a, recv_a, send_b, recv_b, send_c, recv_c, send_d, recv_d, send_e, recv_e, send_f, recv_f,
    ) = scratch
    me = (lax.axis_index("gx"), lax.axis_index("gy"), lax.axis_index("gz"))
    counts = (COUNT_X, COUNT_Y, COUNT_Z)

    def at(offset):
        return tuple(lax.rem(m + o + c, c) for m, o, c in zip(me, offset, counts))

    def remote(source, target, sends, recvs, index, offset):
        return pltpu.make_async_remote_copy(
            src_ref=source, dst_ref=target, send_sem=sends.at[index], recv_sem=recvs.at[index],
            device_id=at(offset), device_id_type=MESH,
        )

    def launch(copies):
        for copy in copies:
            copy.start()

    def sent(copies):
        for copy in copies:
            copy.wait_send()

    def arrive(copies):
        for copy in copies:
            copy.wait_recv()

    loads = [pltpu.make_async_copy(magnetic.at[c], field.at[c], load_sem.at[c]) for c in range(3)]
    for load in loads:
        load.start()
    barrier = pltpu.get_barrier_semaphore()
    for offset in GREETED:
        pl.semaphore_signal(barrier, inc=1, device_id=at(offset), device_id_type=MESH)
    for load in loads:
        load.wait()

    lane32 = lane_of((32, 128))
    row32 = row_of((32, 128))

    last_y[...] = field[1, pl.ds(31, 16, stride=32), :]
    column = jnp.zeros((32, 128), F32)
    for x in range(16):
        column = jnp.where(
            lane32 == x, turned(field[2, x * 32 : x * 32 + 32, :], x + 1, 1), column
        )
    last_z[...] = column
    pl.semaphore_wait(barrier, len(GREETED))
    round_a = [
        remote(field.at[0, pl.ds(480, 32)], low_x, send_a, recv_a, 0, (1, 0, 0)),
        remote(last_y, low_y, send_a, recv_a, 1, (0, 1, 0)),
        remote(last_z, low_z, send_a, recv_a, 2, (0, 0, 1)),
    ]
    launch(round_a)
    for offset in ((-1, 0, 0), (0, -1, 0), (0, 0, -1)):
        pl.semaphore_signal(enter_sem, inc=1, device_id=at(offset), device_id_type=MESH)
    pl.semaphore_wait(enter_sem, 3)
    arrive(round_a)

    column = low_z[...]
    halves = []
    edge = (lane32 < 8) | (lane32 >= 120)
    for half in range(2):
        total = jnp.zeros((32, 128), F32)
        for slot in range(8):
            x = half * 8 + slot
            own_x = field[0, x * 32 : x * 32 + 32, :]
            below_x = low_x[...] if x == 0 else field[0, x * 32 - 32 : x * 32, :]
            own_y = field[1, x * 32 : x * 32 + 32, :]
            below_y = jnp.where(row32 == 0, low_y[x : x + 1, :], turned(own_y, 1, 0))
            own_z = field[2, x * 32 : x * 32 + 32, :]
            below_z = jnp.where(lane32 == 0, turned(column, -x, 1), turned(own_z, 1, 1))
            value = ((below_x - own_x) + (below_y - own_y) + (below_z - own_z)) * SEVENTH
            source0[6 + x, 8:40, 0:128] = value
            total = total + turned(jnp.where(edge, value, 0.0), slot * 16, 1)
        packed0[:, half * 128 : half * 128 + 128] = total

    rows_from = {-1: (24, 8), 0: (0, 32), 1: (0, 8)}
    rows_to = {-1: 0, 0: 8, 1: 40}
    planes_from = {-1: (10, 6), 0: (0, 16), 1: (0, 6)}
    planes_to = {-1: 0, 0: 6, 1: 22}
    lanes_from = {-1: (128, 128), 0: (0, 256), 1: (0, 128)}
    lanes_to = {-1: 0, 0: 128, 1: 384}
    round_b = []
    for index, (dx, dy, dz) in enumerate(BULKY):
        (row, rows), peer = rows_from[dy], (-dx, -dy, -dz)
        if dz == 0:
            plane, planes = planes_from[dx]
            origin = source0.at[pl.ds(6 + plane, planes), pl.ds(8 + row, rows), pl.ds(0, 128)]
            target = source0.at[pl.ds(planes_to[dx], planes), pl.ds(rows_to[dy], rows), pl.ds(0, 128)]
        else:
            lane, lanes = lanes_from[dx]
            origin = packed0.at[pl.ds(row, rows), pl.ds(lane, lanes)]
            target = sides0.at[(dz + 1) // 2, pl.ds(rows_to[dy], rows), pl.ds(lanes_to[dx], lanes)]
        round_b.append(remote(origin, target, send_b, recv_b, index, peer))
    launch(round_b)
    sent(round_a)
    halve0[...] = halving(64)
    halve1[...] = halving(32)
    halve2[...] = halving(16)
    straight[...] = doubling(256, False)
    wrapped[...] = doubling(128, True)
    arrive(round_b)

    lane48 = lane_of((48, 128))
    for group in range(4):
        lanes = slice(group * 128, group * 128 + 128)
        joined = jnp.where((lane48 // 8) % 2 == 1, sides0[0, :, lanes], sides0[1, :, lanes])
        for slot in range(8):
            x = group * 8 + slot - 8
            if -6 <= x < 22:
                source0[6 + x, :, 128:256] = turned(joined, -16 * slot, 1)
    sweep(first0, source0, source0, 4, 24, 2)
    sweep(second0, first0, source0, 5, 23, 2)

    def restrict0(index, carry):
        pairs0[index] = residual_pair(second0, source0, 6 + 2 * index)[8:40, 0:128]
        return carry

    lax.fori_loop(0, 8, restrict0, 0, unroll=True)

    coarse = selected(row_pairs(pairs0, 8, 16), halve0[...]).reshape(8, 16, 128)
    lane16 = lane_of((16, 128))
    for x in range(4):
        slabs1[1, x, 8:24, :] = jnp.where(lane16 < 64, coarse[x], coarse[x + 4])
    edge = ((lane16 >= 64) & (lane16 < 72)) | (lane16 >= 120)
    total = jnp.zeros((16, 128), F32)
    for x in range(8):
        total = total + turned(jnp.where(edge, coarse[x], 0.0), 16 * x + 8, 1)
    packed1[...] = total
    rows_from = {-1: (8, 8), 0: (0, 16), 1: (0, 8)}
    rows_to = {-1: 0, 0: 8, 1: 24}
    round_c = []
    for index, (dx, dy, dz) in enumerate(NEAR):
        (row, rows), peer = rows_from[dy], (-dx, -dy, -dz)
        if dz == 0:
            origin = slabs1.at[1, :, pl.ds(8 + row, rows), :]
            target = slabs1.at[dx + 1, :, pl.ds(rows_to[dy], rows), :]
        else:
            origin = packed1.at[pl.ds(row, rows), :]
            target = sides1.at[(dz + 1) // 2, dx + 1, pl.ds(rows_to[dy], rows), :]
        round_c.append(remote(origin, target, send_c, recv_c, index, peer))
    launch(round_c)
    sent(round_b)
    sweep(first0, source0, source0, 1, 4, 3)
    sweep(first0, source0, source0, 24, 27, 3)
    sweep(second0, first0, source0, 2, 5, 3)
    sweep(second0, first0, source0, 23, 26, 3)
    arrive(round_c)
    for group in range(3):
        joined = jnp.where((lane32 // 8) % 2 == 0, sides1[0, group], sides1[1, group])
        for x in range(8):
            main = slabs1[group, x % 4]
            if x >= 4:
                main = turned(main, 64, 1)
            side = turned(joined, -(16 * x + 8), 1)
            source1[group * 8 + x] = jnp.where(lane32 < 64, main, side)
    sweep(first1, source1, source1, 6, 18, 4)
    sweep(second1, first1, source1, 7, 17, 5)
    for index in range(4):
        pairs1[index] = residual_pair(second1, source1, 8 + 2 * index)[8:24, :]

    coarse = selected(row_pairs(pairs1, 4, 8), halve1[...]).reshape(4, 8, 128)
    group8 = lane_of((8, 128)) // 32
    for step in (-1, 0, 1):
        total = coarse[3]
        for x in range(3):
            total = jnp.where(group8 == (x + step) % 4, coarse[x], total)
        if step == 0:
            blocks2[1, 2, 8:16, :] = total
        else:
            packed2[(step + 1) // 2] = total
    round_d = []
    for index, (dx, dy, dz) in enumerate(NEAR + WIDE):
        origin = blocks2.at[1, 2, pl.ds(8, 8), :] if dz == 0 else packed2.at[(dz + 1) // 2]
        target = blocks2.at[dz + 1, dx + 2, pl.ds(8 * dy + 8, 8), :]
        round_d.append(remote(origin, target, send_d, recv_d, index, (-dx, -dy, -dz)))
    launch(round_d)
    sent(round_c)
    sweep(first1, source1, source1, 1, 6, 5)
    sweep(first1, source1, source1, 18, 23, 5)
    sweep(second1, first1, source1, 2, 7, 5)
    sweep(second1, first1, source1, 17, 22, 5)
    arrive(round_d[: len(NEAR)])
    group24 = lane_of((24, 128)) // 32

    def unpack2(block):
        for x in range(4):
            value = jnp.where(group24 == (x + 1) % 4, blocks2[2, block], blocks2[0, block])
            value = jnp.where(group24 == x, blocks2[1, block], value)
            source2[block * 4 + x] = turned(value, -32 * x, 1)

    for block in (1, 2, 3):
        unpack2(block)
    sweep(first2, source2, source2, 6, 14, 4)
    sweep(second2, first2, source2, 7, 13, 6)
    for index in range(2):
        pairs2[index] = residual_pair(second2, source2, 8 + 2 * index)[8:16, :]

    lines3[0] = selected(row_pairs(pairs2, 2, 4), halve2[...])
    round_e = [
        remote(lines3.at[0], lines3.at[z], send_e, recv_e, z - 1, (0, 0, -z)) for z in LINE
    ]
    launch(round_e)
    sent(round_d)
    arrive(round_d[len(NEAR) :])
    unpack2(0)
    unpack2(4)
    sweep(first2, source2, source2, 1, 6, 5)
    sweep(first2, source2, source2, 14, 19, 5)
    sweep(second2, first2, source2, 2, 7, 5)
    sweep(second2, first2, source2, 13, 18, 5)
    arrive(round_e)
    group8 = lane_of((8, 128)) // 16
    line = lines3[0]
    for z in range(1, COUNT_Z):
        line = jnp.where(group8 == z, lines3[z], line)
    gathered3[0, 0] = line
    round_f = [
        remote(gathered3.at[0, 0], gathered3.at[a, b], send_f, recv_f, index, (-a, -b, 0))
        for index, (a, b) in enumerate(PLANE)
    ]
    launch(round_f)
    sent(round_e)
    arrive(round_f)
    for a in range(COUNT_X):
        for b in range(COUNT_Y):
            for x in range(2):
                source3[2 * a + x, 4 * b : 4 * b + 4, :] = gathered3[a, b, 4 * x : 4 * x + 4, :]

    def mixed_whole(value):
        below = jnp.concatenate([value[-1:], value[:-1]], axis=0)
        above = jnp.concatenate([value[1:], value[:1]], axis=0)
        return mixed(value, below, above)

    right = source3[...]
    value = right
    for repeat in range(SWEEPS - 1):
        value = mixed_whole(value) + right
    rest = mixed_whole(value) + right - value
    level3[...] = value
    rest = rest.reshape(8, 2, 16, 128)
    pairs3[...] = rest[:, 0] + rest[:, 1]

    coarse = selected(row_pairs(pairs3, 8, 8), halve0[...]).reshape(8, 8, 128)
    error = lax.fori_loop(
        0,
        COARSE_ITERS - 1,
        lambda index, current: mixed_whole(current) + coarse,
        coarse,
        unroll=True,
    )

    spread = selected(error.reshape(64, 128), straight[:, 0:128]).reshape(8, 8, 128)
    for x in range(8):
        pairs3[x, pl.ds(0, 8, stride=2), :] = spread[x]
        pairs3[x, pl.ds(1, 8, stride=2), :] = spread[x]
    spread = jnp.broadcast_to(pairs3[...][:, None], (8, 2, 16, 128)).reshape(16, 16, 128)
    value = level3[...] + spread
    value = jnp.concatenate([value[10:16], value[0:8]], axis=0)
    right = jnp.concatenate([right[10:16], right[0:8]], axis=0)
    for repeat in range(SWEEPS):
        right = right[1:-1]
        value = mixed(value[1:-1], value[:-2], value[2:]) + right

    near = value
    near = turned(near, 4, 1)
    spread = selected(near.reshape(128, 128), wrapped[...]).reshape(8, 16, 128)
    for x in range(8):
        spread2[x, pl.ds(0, 12, stride=2), :] = spread[x, 0:12]
        spread2[x, pl.ds(1, 12, stride=2), :] = spread[x, 0:12]
    for x in range(8):
        for side in range(2):
            second2[2 + 2 * x + side] = second2[2 + 2 * x + side] + spread2[x]
    sweep(first2, second2, source2, 3, 17, 7)
    sweep(second2, first2, source2, 4, 16, 6)
    sweep(first2, second2, source2, 5, 15, 5)

    near = first2[5:15, 4:20, :]
    spread = selected(near.reshape(160, 128), wrapped[...]).reshape(10, 16, 128)
    for x in range(10):
        spread1[x, pl.ds(0, 16, stride=2), :] = spread[x]
        spread1[x, pl.ds(1, 16, stride=2), :] = spread[x]
    for x in range(10):
        for side in range(2):
            second1[2 + 2 * x + side] = second1[2 + 2 * x + side] + spread1[x]
    sweep(first1, second1, source1, 3, 21, 3)
    sweep(second1, first1, source1, 4, 20, 4)
    sweep(first1, second1, source1, 5, 19, 2)

    near = first1[6:18, 4:28, :]
    spread = selected(near.reshape(288, 128), straight[...]).reshape(12, 24, 256)
    for x in range(12):
        for half in range(2):
            lanes = slice(half * 128, half * 128 + 128)
            spread0[half, x, pl.ds(0, 24, stride=2), :] = spread[x, :, lanes]
            spread0[half, x, pl.ds(1, 24, stride=2), :] = spread[x, :, lanes]

    def correct0(index, carry):
        for half in range(2):
            lanes = slice(half * 128, half * 128 + 128)
            for side in range(2):
                x = 2 + 2 * index + side
                second0[x, :, lanes] = second0[x, :, lanes] + spread0[half, index]
        return carry

    lax.fori_loop(0, 12, correct0, 0, unroll=True)
    sweep(first0, second0, source0, 3, 25, 2)
    sweep(second0, first0, source0, 4, 24, 2)
    sweep(first0, second0, source0, 5, 23, 2)

    def finish(x, carry):
        whole = first0[6 + x]
        here = whole[8:40, 0:128]
        above_x = first0[7 + x, 8:40, 0:128]
        above_y = turned(whole[:, 0:128], -1, 0)[8:40]
        above_z = turned(whole[8:40], -1, 1)[:, 0:128]
        rows = pl.ds(pl.multiple_of(x * 32, 32), 32)
        result[0, rows, :] = field[0, rows, :] - (above_x - here)
        result[1, rows, :] = field[1, rows, :] - (above_y - here)
        result[2, rows, :] = field[2, rows, :] - (above_z - here)
        return carry

    lax.fori_loop(0, 16, finish, 0, unroll=True)
    sent(round_f)


def scratch_shapes():
    def vmem(*shape):
        return pltpu.VMEM(shape, F32)

    def half(lanes):
        return pltpu.VMEM((128, lanes), jnp.bfloat16)

    dma = pltpu.SemaphoreType.DMA
    return [
        vmem(3, 512, 128), vmem(32, 128), vmem(16, 128), vmem(32, 128), vmem(16, 128), vmem(32, 128),
        vmem(28, 48, 256), vmem(28, 48, 256), vmem(28, 48, 256), vmem(32, 256), vmem(2, 48, 512), vmem(8, 32, 128), vmem(2, 12, 48, 128),
        vmem(3, 4, 32, 128), vmem(16, 128), vmem(2, 3, 32, 128), vmem(24, 32, 128), vmem(24, 32, 128), vmem(24, 32, 128), vmem(4, 16, 128), vmem(10, 32, 128),
        vmem(2, 8, 128), vmem(3, 5, 24, 128), vmem(20, 24, 128), vmem(20, 24, 128), vmem(20, 24, 128), vmem(2, 8, 128), vmem(8, 24, 128),
        vmem(8, 8, 128), vmem(8, 4, 8, 128), vmem(16, 16, 128), vmem(16, 16, 128), vmem(8, 16, 128),
        half(128), half(128), half(128), half(256), half(128),
        dma((3,)), pltpu.SemaphoreType.REGULAR,
        dma((3,)), dma((3,)), dma((26,)), dma((26,)), dma((26,)), dma((26,)), dma((44,)), dma((44,)), dma((7,)), dma((7,)), dma((31,)), dma((31,)),
    ]


def body(magnetic):
    cleaned = pl.pallas_call(
        kernel,
        out_shape=jax.ShapeDtypeStruct((3, 512, 128), F32),
        in_specs=[pl.BlockSpec(memory_space=pl.ANY)],
        out_specs=pl.BlockSpec(memory_space=pltpu.VMEM),
        scratch_shapes=scratch_shapes(),
        compiler_params=pltpu.CompilerParams(
            collective_id=0, has_side_effects=True, vmem_limit_bytes=53 << 20
        ),
    )(magnetic.reshape(3, 512, 128))
    return cleaned.reshape(3, 16, 32, 128)


def solution(mesh):
    spec = P(None, "gx", "gy", "gz")
    return jax.shard_map(body, mesh=mesh, in_specs=(spec,), out_specs=spec, check_vma=False)
```

```python
import itertools

import jax
import jax.numpy as jnp
from jax import lax
from jax.experimental import pallas as pl
from jax.experimental.pallas import tpu as pltpu
from jax.sharding import PartitionSpec as P

SWEEPS = 3
COARSE_ITERS = 24
MESH = pl.DeviceIdType.MESH
F32 = jnp.float32
COUNT_X, COUNT_Y, COUNT_Z = 8, 4, 8
NEAR = sorted(
    (d for d in itertools.product((-1, 0, 1), repeat=3) if d != (0, 0, 0)),
    key=lambda d: -sum(map(abs, d)),
)
GREETED = [d for d in reversed(NEAR) if sum(map(abs, d)) != 2]
BULKY = sorted(NEAR, key=lambda d: d not in [(0, 1, 0), (0, -1, 0), (1, 0, 0), (-1, 0, 0)])
WIDE = [(dx, dy, dz) for dx in (-2, 2) for dy in (-1, 0, 1) for dz in (-1, 0, 1)]
LINE = sorted(range(1, COUNT_Z), key=lambda z: -min(z, COUNT_Z - z))
PLANE = sorted(
    ((a, b) for a in range(COUNT_X) for b in range(COUNT_Y) if (a, b) != (0, 0)),
    key=lambda d: -min(d[0], COUNT_X - d[0]) - 2 * min(d[1], COUNT_Y - d[1]),
)
SEVENTH = 1.0 / 7.0


def lane_of(shape):
    return lax.broadcasted_iota(jnp.int32, shape, len(shape) - 1)


def row_of(shape):
    return lax.broadcasted_iota(jnp.int32, shape, len(shape) - 2)


def turned(value, shift, axis):
    shift = shift % value.shape[axis]
    return value if shift == 0 else pltpu.roll(value, shift, axis)


def mixed(center, low, high):
    rows, lanes = center.ndim - 2, center.ndim - 1
    total = center + low + high
    total = total + (turned(center, 1, rows) + turned(center, -1, rows))
    total = total + (turned(center, 1, lanes) + turned(center, -1, lanes))
    return total * SEVENTH


def sweep(target, current, source, low, high, step):
    def body(index, carry):
        at = low + index * step
        mean = mixed(
            current[pl.ds(at, step)], current[pl.ds(at - 1, step)], current[pl.ds(at + 1, step)]
        )
        target[pl.ds(at, step)] = mean + source[pl.ds(at, step)]
        return carry

    lax.fori_loop(0, (high - low) // step, body, 0, unroll=True)


def residual_pair(current, source, at):
    center = current[pl.ds(at, 2)]
    mean = mixed(center, current[pl.ds(at - 1, 2)], current[pl.ds(at + 1, 2)])
    value = mean + source[pl.ds(at, 2)] - center
    return value[0] + value[1]


def selected(value, matrix):
    total = None
    for term in range(3):
        part = value.astype(jnp.bfloat16)
        value = value - part.astype(F32)
        product = jnp.dot(part, matrix, preferred_element_type=F32)
        total = product if total is None else total + product
    return total


def halving(period):
    lane, row = lane_of((128, 128)), row_of((128, 128))
    return jnp.where(row // 2 == lane % period, 0.5, 0.0).astype(jnp.bfloat16)


def doubling(lanes, wrap):
    lane, row = lane_of((128, lanes)), row_of((128, lanes))
    origin = lane // 2
    if wrap:
        origin = origin + jnp.where(lane >= 96, 64, 0)
    return jnp.where(row == origin, 1.0, 0.0).astype(jnp.bfloat16)


def row_pairs(ref, count, rows):
    pieces = [
        ref[index, pl.ds(0, rows, stride=2), :] + ref[index, pl.ds(1, rows, stride=2), :]
        for index in range(count)
    ]
    return jnp.concatenate(pieces, axis=0)


def kernel(magnetic, result, *scratch):
    (
        field, low_x, low_y, low_z, last_y, last_z,
        source0, first0, second0, packed0, sides0, pairs0, spread0,
        slabs1, packed1, sides1, source1, first1, second1, pairs1, spread1,
        packed2, blocks2, source2, first2, second2, pairs2, spread2,
        lines3, gathered3, source3, level3, pairs3,
        halve0, halve1, halve2, straight, wrapped,
        load_sem, enter_sem,
        send_a, recv_a, send_b, recv_b, send_c, recv_c, send_d, recv_d, send_e, recv_e, send_f, recv_f,
    ) = scratch
    me = (lax.axis_index("gx"), lax.axis_index("gy"), lax.axis_index("gz"))
    counts = (COUNT_X, COUNT_Y, COUNT_Z)

    def at(offset):
        return tuple(lax.rem(m + o + c, c) for m, o, c in zip(me, offset, counts))

    def remote(source, target, sends, recvs, index, offset):
        return pltpu.make_async_remote_copy(
            src_ref=source, dst_ref=target, send_sem=sends.at[index], recv_sem=recvs.at[index],
            device_id=at(offset), device_id_type=MESH,
        )

    def launch(copies):
        for copy in copies:
            copy.start()

    def sent(copies):
        for copy in copies:
            copy.wait_send()

    def arrive(copies):
        for copy in copies:
            copy.wait_recv()

    loads = [pltpu.make_async_copy(magnetic.at[c], field.at[c], load_sem.at[c]) for c in range(3)]
    for load in loads:
        load.start()
    barrier = pltpu.get_barrier_semaphore()
    for offset in GREETED:
        pl.semaphore_signal(barrier, inc=1, device_id=at(offset), device_id_type=MESH)
    for load in loads:
        load.wait()

    lane32 = lane_of((32, 128))
    row32 = row_of((32, 128))

    last_y[...] = field[1, pl.ds(31, 16, stride=32), :]
    column = jnp.zeros((32, 128), F32)
    for x in range(16):
        column = jnp.where(
            lane32 == x, turned(field[2, x * 32 : x * 32 + 32, :], x + 1, 1), column
        )
    last_z[...] = column
    pl.semaphore_wait(barrier, len(GREETED))
    round_a = [
        remote(field.at[0, pl.ds(480, 32)], low_x, send_a, recv_a, 0, (1, 0, 0)),
        remote(last_y, low_y, send_a, recv_a, 1, (0, 1, 0)),
        remote(last_z, low_z, send_a, recv_a, 2, (0, 0, 1)),
    ]
    launch(round_a)
    for offset in ((-1, 0, 0), (0, -1, 0), (0, 0, -1)):
        pl.semaphore_signal(enter_sem, inc=1, device_id=at(offset), device_id_type=MESH)
    pl.semaphore_wait(enter_sem, 3)
    arrive(round_a)

    column = low_z[...]
    halves = []
    edge = (lane32 < 8) | (lane32 >= 120)
    for half in range(2):
        total = jnp.zeros((32, 128), F32)
        for slot in range(8):
            x = half * 8 + slot
            own_x = field[0, x * 32 : x * 32 + 32, :]
            below_x = low_x[...] if x == 0 else field[0, x * 32 - 32 : x * 32, :]
            own_y = field[1, x * 32 : x * 32 + 32, :]
            below_y = jnp.where(row32 == 0, low_y[x : x + 1, :], turned(own_y, 1, 0))
            own_z = field[2, x * 32 : x * 32 + 32, :]
            below_z = jnp.where(lane32 == 0, turned(column, -x, 1), turned(own_z, 1, 1))
            value = ((below_x - own_x) + (below_y - own_y) + (below_z - own_z)) * SEVENTH
            source0[6 + x, 8:40, 0:128] = value
            total = total + turned(jnp.where(edge, value, 0.0), slot * 16, 1)
        packed0[:, half * 128 : half * 128 + 128] = total

    rows_from = {-1: (24, 8), 0: (0, 32), 1: (0, 8)}
    rows_to = {-1: 0, 0: 8, 1: 40}
    planes_from = {-1: (11, 5), 0: (0, 16), 1: (0, 6)}
    planes_to = {-1: 1, 0: 6, 1: 22}
    lanes_from = {-1: (128, 128), 0: (0, 256), 1: (0, 128)}
    lanes_to = {-1: 0, 0: 128, 1: 384}
    round_b = []
    for index, (dx, dy, dz) in enumerate(BULKY):
        (row, rows), peer = rows_from[dy], (-dx, -dy, -dz)
        if dz == 0:
            plane, planes = planes_from[dx]
            origin = source0.at[pl.ds(6 + plane, planes), pl.ds(8 + row, rows), pl.ds(0, 128)]
            target = source0.at[pl.ds(planes_to[dx], planes), pl.ds(rows_to[dy], rows), pl.ds(0, 128)]
        else:
            lane, lanes = lanes_from[dx]
            origin = packed0.at[pl.ds(row, rows), pl.ds(lane, lanes)]
            target = sides0.at[(dz + 1) // 2, pl.ds(rows_to[dy], rows), pl.ds(lanes_to[dx], lanes)]
        round_b.append(remote(origin, target, send_b, recv_b, index, peer))
    launch(round_b)
    sent(round_a)
    halve0[...] = halving(64)
    halve1[...] = halving(32)
    halve2[...] = halving(16)
    straight[...] = doubling(256, False)
    wrapped[...] = doubling(128, True)
    arrive(round_b)

    lane48 = lane_of((48, 128))
    for group in range(4):
        lanes = slice(group * 128, group * 128 + 128)
        joined = jnp.where((lane48 // 8) % 2 == 1, sides0[0, :, lanes], sides0[1, :, lanes])
        for slot in range(8):
            x = group * 8 + slot - 8
            if -5 <= x < 22:
                source0[6 + x, :, 128:256] = turned(joined, -16 * slot, 1)
    sweep(first0, source0, source0, 4, 24, 2)
    sweep(second0, first0, source0, 5, 23, 2)

    def restrict0(index, carry):
        pairs0[index] = residual_pair(second0, source0, 6 + 2 * index)[8:40, 0:128]
        return carry

    lax.fori_loop(0, 8, restrict0, 0, unroll=True)

    coarse = selected(row_pairs(pairs0, 8, 16), halve0[...]).reshape(8, 16, 128)
    lane16 = lane_of((16, 128))
    for x in range(4):
        slabs1[1, x, 8:24, :] = jnp.where(lane16 < 64, coarse[x], coarse[x + 4])
    edge = ((lane16 >= 64) & (lane16 < 72)) | (lane16 >= 120)
    total = jnp.zeros((16, 128), F32)
    for x in range(8):
        total = total + turned(jnp.where(edge, coarse[x], 0.0), 16 * x + 8, 1)
    packed1[...] = total
    rows_from = {-1: (8, 8), 0: (0, 16), 1: (0, 8)}
    rows_to = {-1: 0, 0: 8, 1: 24}
    round_c = []
    for index, (dx, dy, dz) in enumerate(NEAR):
        (row, rows), peer = rows_from[dy], (-dx, -dy, -dz)
        if dz == 0:
            origin = slabs1.at[1, :, pl.ds(8 + row, rows), :]
            target = slabs1.at[dx + 1, :, pl.ds(rows_to[dy], rows), :]
        else:
            origin = packed1.at[pl.ds(row, rows), :]
            target = sides1.at[(dz + 1) // 2, dx + 1, pl.ds(rows_to[dy], rows), :]
        round_c.append(remote(origin, target, send_c, recv_c, index, peer))
    launch(round_c)
    sent(round_b)
    sweep(first0, source0, source0, 2, 4, 2)
    sweep(first0, source0, source0, 24, 27, 3)
    sweep(second0, first0, source0, 3, 5, 2)
    sweep(second0, first0, source0, 23, 26, 3)
    arrive(round_c)
    for group in range(3):
        joined = jnp.where((lane32 // 8) % 2 == 0, sides1[0, group], sides1[1, group])
        for x in range(8):
            main = slabs1[group, x % 4]
            if x >= 4:
                main = turned(main, 64, 1)
            side = turned(joined, -(16 * x + 8), 1)
            source1[group * 8 + x] = jnp.where(lane32 < 64, main, side)
    sweep(first1, source1, source1, 6, 18, 4)
    sweep(second1, first1, source1, 7, 17, 5)
    for index in range(4):
        pairs1[index] = residual_pair(second1, source1, 8 + 2 * index)[8:24, :]

    coarse = selected(row_pairs(pairs1, 4, 8), halve1[...]).reshape(4, 8, 128)
    group8 = lane_of((8, 128)) // 32
    for step in (-1, 0, 1):
        total = coarse[3]
        for x in range(3):
            total = jnp.where(group8 == (x + step) % 4, coarse[x], total)
        if step == 0:
            blocks2[1, 2, 8:16, :] = total
        else:
            packed2[(step + 1) // 2] = total
    round_d = []
    for index, (dx, dy, dz) in enumerate(NEAR + WIDE):
        origin = blocks2.at[1, 2, pl.ds(8, 8), :] if dz == 0 else packed2.at[(dz + 1) // 2]
        target = blocks2.at[dz + 1, dx + 2, pl.ds(8 * dy + 8, 8), :]
        round_d.append(remote(origin, target, send_d, recv_d, index, (-dx, -dy, -dz)))
    launch(round_d)
    sent(round_c)
    sweep(first1, source1, source1, 1, 6, 5)
    sweep(first1, source1, source1, 18, 23, 5)
    sweep(second1, first1, source1, 2, 7, 5)
    sweep(second1, first1, source1, 17, 22, 5)
    arrive(round_d[: len(NEAR)])
    group24 = lane_of((24, 128)) // 32

    def unpack2(block):
        for x in range(4):
            value = jnp.where(group24 == (x + 1) % 4, blocks2[2, block], blocks2[0, block])
            value = jnp.where(group24 == x, blocks2[1, block], value)
            source2[block * 4 + x] = turned(value, -32 * x, 1)

    for block in (1, 2, 3):
        unpack2(block)
    sweep(first2, source2, source2, 6, 14, 4)
    sweep(second2, first2, source2, 7, 13, 6)
    for index in range(2):
        pairs2[index] = residual_pair(second2, source2, 8 + 2 * index)[8:16, :]

    lines3[0] = selected(row_pairs(pairs2, 2, 4), halve2[...])
    round_e = [
        remote(lines3.at[0], lines3.at[z], send_e, recv_e, z - 1, (0, 0, -z)) for z in LINE
    ]
    launch(round_e)
    sent(round_d)
    arrive(round_d[len(NEAR) :])
    unpack2(0)
    unpack2(4)
    sweep(first2, source2, source2, 1, 6, 5)
    sweep(first2, source2, source2, 14, 19, 5)
    sweep(second2, first2, source2, 2, 7, 5)
    sweep(second2, first2, source2, 13, 18, 5)
    arrive(round_e)
    group8 = lane_of((8, 128)) // 16
    line = lines3[0]
    for z in range(1, COUNT_Z):
        line = jnp.where(group8 == z, lines3[z], line)
    gathered3[0, 0] = line
    round_f = [
        remote(gathered3.at[0, 0], gathered3.at[a, b], send_f, recv_f, index, (-a, -b, 0))
        for index, (a, b) in enumerate(PLANE)
    ]
    launch(round_f)
    sent(round_e)
    arrive(round_f)
    for a in range(COUNT_X):
        for b in range(COUNT_Y):
            for x in range(2):
                source3[2 * a + x, 4 * b : 4 * b + 4, :] = gathered3[a, b, 4 * x : 4 * x + 4, :]

    def mixed_whole(value):
        below = jnp.concatenate([value[-1:], value[:-1]], axis=0)
        above = jnp.concatenate([value[1:], value[:1]], axis=0)
        return mixed(value, below, above)

    right = source3[...]
    value = right
    for repeat in range(SWEEPS - 1):
        value = mixed_whole(value) + right
    rest = mixed_whole(value) + right - value
    level3[...] = value
    rest = rest.reshape(8, 2, 16, 128)
    pairs3[...] = rest[:, 0] + rest[:, 1]

    coarse = selected(row_pairs(pairs3, 8, 8), halve0[...]).reshape(8, 8, 128)
    error = lax.fori_loop(
        0,
        COARSE_ITERS - 1,
        lambda index, current: mixed_whole(current) + coarse,
        coarse,
        unroll=True,
    )

    spread = selected(error.reshape(64, 128), straight[:, 0:128]).reshape(8, 8, 128)
    for x in range(8):
        pairs3[x, pl.ds(0, 8, stride=2), :] = spread[x]
        pairs3[x, pl.ds(1, 8, stride=2), :] = spread[x]
    spread = jnp.broadcast_to(pairs3[...][:, None], (8, 2, 16, 128)).reshape(16, 16, 128)
    value = level3[...] + spread
    value = jnp.concatenate([value[10:16], value[0:8]], axis=0)
    right = jnp.concatenate([right[10:16], right[0:8]], axis=0)
    for repeat in range(SWEEPS):
        right = right[1:-1]
        value = mixed(value[1:-1], value[:-2], value[2:]) + right

    near = value
    near = turned(near, 4, 1)
    spread = selected(near.reshape(128, 128), wrapped[...]).reshape(8, 16, 128)
    for x in range(8):
        spread2[x, pl.ds(0, 12, stride=2), :] = spread[x, 0:12]
        spread2[x, pl.ds(1, 12, stride=2), :] = spread[x, 0:12]
    for x in range(8):
        for side in range(2):
            second2[2 + 2 * x + side] = second2[2 + 2 * x + side] + spread2[x]
    sweep(first2, second2, source2, 3, 17, 7)
    sweep(second2, first2, source2, 4, 16, 6)
    sweep(first2, second2, source2, 5, 15, 5)

    near = first2[5:15, 4:20, :]
    spread = selected(near.reshape(160, 128), wrapped[...]).reshape(10, 16, 128)
    for x in range(10):
        spread1[x, pl.ds(0, 16, stride=2), :] = spread[x]
        spread1[x, pl.ds(1, 16, stride=2), :] = spread[x]
    for x in range(10):
        for side in range(2):
            second1[2 + 2 * x + side] = second1[2 + 2 * x + side] + spread1[x]
    sweep(first1, second1, source1, 3, 21, 3)
    sweep(second1, first1, source1, 4, 20, 4)
    sweep(first1, second1, source1, 5, 19, 2)

    near = first1[6:18, 4:28, :]
    spread = selected(near.reshape(288, 128), straight[...]).reshape(12, 24, 256)
    for x in range(12):
        for half in range(2):
            lanes = slice(half * 128, half * 128 + 128)
            spread0[half, x, pl.ds(0, 24, stride=2), :] = spread[x, :, lanes]
            spread0[half, x, pl.ds(1, 24, stride=2), :] = spread[x, :, lanes]

    def correct0(index, carry):
        for half in range(2):
            lanes = slice(half * 128, half * 128 + 128)
            for side in range(2):
                x = 2 + 2 * index + side
                second0[x, :, lanes] = second0[x, :, lanes] + spread0[half, index]
        return carry

    lax.fori_loop(0, 12, correct0, 0, unroll=True)
    sweep(first0, second0, source0, 4, 25, 3)
    sweep(second0, first0, source0, 5, 24, 1)
    sweep(first0, second0, source0, 6, 23, 1)

    def finish(x, carry):
        whole = first0[6 + x]
        here = whole[8:40, 0:128]
        above_x = first0[7 + x, 8:40, 0:128]
        above_y = turned(whole[:, 0:128], -1, 0)[8:40]
        above_z = turned(whole[8:40], -1, 1)[:, 0:128]
        rows = pl.ds(pl.multiple_of(x * 32, 32), 32)
        result[0, rows, :] = field[0, rows, :] - (above_x - here)
        result[1, rows, :] = field[1, rows, :] - (above_y - here)
        result[2, rows, :] = field[2, rows, :] - (above_z - here)
        return carry

    lax.fori_loop(0, 16, finish, 0, unroll=True)
    sent(round_f)


def scratch_shapes():
    def vmem(*shape):
        return pltpu.VMEM(shape, F32)

    def half(lanes):
        return pltpu.VMEM((128, lanes), jnp.bfloat16)

    dma = pltpu.SemaphoreType.DMA
    return [
        vmem(3, 512, 128), vmem(32, 128), vmem(16, 128), vmem(32, 128), vmem(16, 128), vmem(32, 128),
        vmem(28, 48, 256), vmem(28, 48, 256), vmem(28, 48, 256), vmem(32, 256), vmem(2, 48, 512), vmem(8, 32, 128), vmem(2, 12, 48, 128),
        vmem(3, 4, 32, 128), vmem(16, 128), vmem(2, 3, 32, 128), vmem(24, 32, 128), vmem(24, 32, 128), vmem(24, 32, 128), vmem(4, 16, 128), vmem(10, 32, 128),
        vmem(2, 8, 128), vmem(3, 5, 24, 128), vmem(20, 24, 128), vmem(20, 24, 128), vmem(20, 24, 128), vmem(2, 8, 128), vmem(8, 24, 128),
        vmem(8, 8, 128), vmem(8, 4, 8, 128), vmem(16, 16, 128), vmem(16, 16, 128), vmem(8, 16, 128),
        half(128), half(128), half(128), half(256), half(128),
        dma((3,)), pltpu.SemaphoreType.REGULAR,
        dma((3,)), dma((3,)), dma((26,)), dma((26,)), dma((26,)), dma((26,)), dma((44,)), dma((44,)), dma((7,)), dma((7,)), dma((31,)), dma((31,)),
    ]


def body(magnetic):
    cleaned = pl.pallas_call(
        kernel,
        out_shape=jax.ShapeDtypeStruct((3, 512, 128), F32),
        in_specs=[pl.BlockSpec(memory_space=pl.ANY)],
        out_specs=pl.BlockSpec(memory_space=pltpu.VMEM),
        scratch_shapes=scratch_shapes(),
        compiler_params=pltpu.CompilerParams(
            collective_id=0, has_side_effects=True, vmem_limit_bytes=53 << 20
        ),
    )(magnetic.reshape(3, 512, 128))
    return cleaned.reshape(3, 16, 32, 128)


def solution(mesh):
    spec = P(None, "gx", "gy", "gz")
    return jax.shard_map(body, mesh=mesh, in_specs=(spec,), out_specs=spec, check_vma=False)
```
